128 devices in a mesh: seq: 8 (over x, core), tensor: 16 (over z, y).
Axes of the slice: x: 4, y: 4, z: 4, core: 2. Of those that a mesh axis runs over, the one named last changes fastest.
Arguments:
- hidden: bfloat16 [1024, 53248], P('seq', 'tensor'), may hold values from -200 to 200, as said below
- down_int: bfloat16 [53248, 16384], P('tensor', 'seq'), may hold values from -8 to 7, as said below
- w_scale: float32 [16384], P('seq'), may hold values from 0.0004 to 0.0025
- had_small: int32 [52, 52], replicated, may hold values from -1 to 1, as said below
Outputs:
- mixed: bfloat16 [1024, 16384], P('tensor', 'seq')
- act_scale: float32 [1024], P('seq')
The draws below stay inside these ranges and needn't reach their ends.
Inputs may be any that keep to these rules, and one draw needn't show every extreme that they name: `hidden`: activations with unequal token and channel scales. `down_int`: whole numbers. A Hadamard matrix: entries -1 or +1 and had_small had_small^T = 52 I.
All inputs are finite; a program needn't handle non-finite values.
Results may differ from the reference program's by a relative error of at most 0.0011.
Values may be sent and summed in bfloat16 or wider, within the bound.
No kernel may reach another device: no remote copies, remote signals or barrier semaphores. Data moves between devices by JAX's collectives and lax.ppermute only.
A program may use at most 192 MiB of HBM per device.

```python
import math
import jax
import jax.numpy as jnp
import numpy as np
from jax import lax

D = 16384
FF = 53248
HAD = 52
BLOCKS = 1024
TOKENS = 1024
N_TENSOR = 16


def draw_hidden(key, part):
    base = jax.random.fold_in(key, 11)
    noise = jnp.clip(jax.random.normal(jax.random.fold_in(base, 1), (TOKENS, FF), jnp.float32), -4.0, 4.0)
    row_scale = jnp.exp(jax.random.uniform(jax.random.fold_in(base, 2), (TOKENS, 1), jnp.float32, jnp.log(0.3), jnp.log(3.0)))
    col_scale = jnp.exp(jax.random.uniform(jax.random.fold_in(base, 3), (1, FF), jnp.float32, jnp.log(0.3), jnp.log(3.0)))
    return (noise * row_scale * col_scale).astype(jnp.bfloat16)


def draw_down_int(key, part):
    values = jax.random.randint(jax.random.fold_in(key, 23), (FF, D), -8, 8, jnp.int32)
    return values.astype(jnp.float32).astype(jnp.bfloat16)


def field_product(left, right):
    left_low, left_high = (left % 5, left // 5)
    right_low, right_high = (right % 5, right // 5)
    low_part = (left_low * right_low + 2 * left_high * right_high) % 5
    high_part = (left_low * right_high + left_high * right_low) % 5
    return low_part + 5 * high_part


def field_difference(left, right):
    return (left % 5 - right % 5) % 5 + 5 * ((left // 5 - right // 5) % 5)


def paley_matrix():
    squares_found = set()
    for element in range(1, 25):
        squares_found.add(field_product(element, element))
    conference = np.zeros((26, 26), np.int64)
    conference[0, 1:] = 1
    conference[1:, 0] = 1
    for row_index in range(25):
        for col_index in range(25):
            gap = field_difference(row_index, col_index)
            if gap == 0:
                conference[row_index + 1, col_index + 1] = 0
            elif gap in squares_found:
                conference[row_index + 1, col_index + 1] = 1
            else:
                conference[row_index + 1, col_index + 1] = -1
    upper_block = np.array([[1, 1], [1, -1]], np.int64)
    lower_block = np.array([[1, -1], [-1, -1]], np.int64)
    return np.kron(conference, upper_block) + np.kron(np.eye(26, dtype=np.int64), lower_block)


def draw_had_small(key, part):
    base_matrix = jnp.asarray(paley_matrix().astype(np.int32))
    row_order = jax.random.permutation(jax.random.fold_in(key, 37), HAD)
    col_order = jax.random.permutation(jax.random.fold_in(key, 41), HAD)
    row_signs = 2 * jax.random.randint(jax.random.fold_in(key, 43), (HAD,), 0, 2, jnp.int32) - 1
    col_signs = 2 * jax.random.randint(jax.random.fold_in(key, 47), (HAD,), 0, 2, jnp.int32) - 1
    permuted = base_matrix[row_order][:, col_order]
    return (row_signs[:, None] * permuted * col_signs[None, :]).astype(jnp.int32)


def block_scale(rng, shape, cuts, least, high):
    level, own = 1.0, jax.random.fold_in(rng, 6)
    for dim, blocks in cuts:
        heights = jnp.exp(jax.random.uniform(jax.random.fold_in(own, dim), (blocks,), jnp.float32, least / len(cuts), high / len(cuts)))
        level = level * jnp.repeat(heights, shape[dim] // blocks).reshape([-1 if axis == dim else 1 for axis in range(len(shape))])
    return level


def setup_inputs(seed: int = 0) -> dict:
    splits = jax.random.split(jax.random.key(seed), 5)
    return {
        "hidden": draw_hidden(jax.random.fold_in(splits[4], 71), 0),
        "down_int": draw_down_int(jax.random.fold_in(splits[4], 71), 0),
        "w_scale": jnp.clip(jnp.exp(math.log(0.0025) - 1.8325815 * jax.random.uniform(splits[2], (D,), jnp.float32) ** block_scale(splits[2], (D,), ((0, 8),), -0.2, 0.2)), 0.0004, 0.0025),
        "had_small": draw_had_small(jax.random.fold_in(splits[4], 71), 0),
    }


clip_ratio = 0.9
epsilon = 1e-05

def sylvester(order):
    left_index = lax.broadcasted_iota(jnp.int32, (order, order), 0)
    right_index = lax.broadcasted_iota(jnp.int32, (order, order), 1)
    both = left_index & right_index
    parity = jnp.zeros((order, order), jnp.int32)
    for shift_bit in range(max(order.bit_length() - 1, 0)):
        parity = parity ^ both >> shift_bit & 1
    return (1 - 2 * parity).astype(jnp.float32)

def reference(hidden, down_int, w_scale, had_small):
    blocked = hidden.astype(jnp.float32).reshape(TOKENS, BLOCKS, HAD)
    first = jnp.einsum('tba,bc->tca', blocked, sylvester(BLOCKS), precision=lax.Precision.HIGHEST)
    second = jnp.einsum('tca,ad->tcd', first, had_small.astype(jnp.float32), precision=lax.Precision.HIGHEST)
    rotated = second.reshape(TOKENS, FF) * jnp.float32(1.0 / math.sqrt(FF))
    peak = lax.optimization_barrier(jnp.max(jnp.abs(rotated), axis=1))
    act_scale = clip_ratio / 7.0 * (peak + epsilon)
    quant = jnp.clip(rotated / act_scale[:, None], -8.0, 7.0)
    width = FF // N_TENSOR

    def accumulate(step, total):
        offset = (step * width).astype(jnp.int32)
        rows_part = lax.dynamic_slice_in_dim(quant, offset, width, 1)
        weight_part = lax.dynamic_slice_in_dim(down_int, offset, width, 0).astype(jnp.float32)
        return total + jnp.dot(rows_part, weight_part, preferred_element_type=jnp.float32, precision=lax.Precision.HIGHEST)
    partial_value = lax.fori_loop(0, N_TENSOR, accumulate, jnp.zeros((TOKENS, D), jnp.float32))
    mixed = (partial_value * act_scale[:, None] * w_scale[None, :]).astype(jnp.bfloat16)
    return (mixed, act_scale)
```

```python
import functools
import math

import jax
import jax.numpy as jnp
from jax import lax
from jax.experimental import pallas as pl
from jax.experimental.pallas import tpu as pltpu
from jax.sharding import PartitionSpec as P

FF = 53248
HAD = 52
CHUNKS = 1

clip_ratio = 0.9
epsilon = 1e-05

F32, BF16, I16, I32 = jnp.float32, jnp.bfloat16, jnp.int16, jnp.int32
LANES = 128
CODE_TOP = 32767.0
SUM_TOP = 32700.0
SLOTS = (0, 1, 3, 2)


def vmem():
    return pl.BlockSpec(memory_space=pltpu.VMEM)


def smem():
    return pl.BlockSpec(memory_space=pltpu.SMEM)


def params(**more):
    return pltpu.CompilerParams(vmem_limit_bytes=60 * 1024 * 1024, **more)


def parity_sign(left, right, bits):
    both = left & right
    parity = jnp.zeros(both.shape, I32)
    for shift_bit in range(bits):
        parity = parity ^ (both >> shift_bit & 1)
    return 1 - 2 * parity


def iota(shape, dim):
    return lax.broadcasted_iota(I32, shape, dim)


def block_of(index):
    return jnp.floor((index.astype(F32) + 0.5) * (1.0 / HAD)).astype(I32)


def rotate_kernel(x_ref, had_ref, code_ref, matrix, mixed):
    width = matrix.shape[0]
    group = 4 * HAD
    row = iota((group, HAD), 0)
    pick_row = (row - HAD * block_of(row) == iota((group, HAD), 1)).astype(BF16)
    lane = iota((HAD, width), 1)
    pick_lane = (lane - HAD * block_of(lane) == iota((HAD, width), 0)).astype(BF16)
    small = had_ref[...].astype(F32).astype(BF16)
    tiled = jnp.dot(small, pick_lane, preferred_element_type=F32).astype(BF16)
    base = jnp.dot(pick_row, tiled, preferred_element_type=F32)
    row_block = block_of(iota((group, width), 0))
    lane_block = block_of(iota((group, width), 1))
    base = base * parity_sign(row_block, lane_block & 3, 2).astype(F32)
    line_block = block_of(iota((8, width), 1)) >> 2
    lines = parity_sign(iota((8, width), 0), line_block, 3).astype(F32)
    for g in range(width // group):
        matrix[g * group : (g + 1) * group, :] = (base * lines[g : g + 1, :]).astype(BF16)
    rows = x_ref.shape[0]
    count = rows // 8
    for half in range(2):
        span = slice(half * width, (half + 1) * width)
        mixed[:, span] = jnp.dot(x_ref[:, span], matrix[...], preferred_element_type=F32)
    norm_factor = jnp.float32(1.0 / math.sqrt(FF))
    top = jnp.zeros((8, LANES), F32)
    for tile in range(width // LANES):
        columns = [slice(half * width + tile * LANES, half * width + (tile + 1) * LANES) for half in range(2)]
        values = [mixed[8 * t : 8 * t + 8, span] for span in columns for t in range(count)]
        step = 1
        while step < len(values):
            for low in range(len(values)):
                if not low & step:
                    a, b = values[low], values[low | step]
                    values[low], values[low | step] = a + b, a - b
            step *= 2
        for index, value in enumerate(values):
            half, t = index // count, index % count
            value = value * norm_factor
            top = jnp.maximum(top, jnp.abs(value))
            mixed[8 * t : 8 * t + 8, columns[half]] = value
    peak = jnp.max(top, axis=1, keepdims=True)
    act_scale = clip_ratio / 7.0 * (peak + epsilon)
    inverse = jnp.broadcast_to(1.0 / act_scale, (8, LANES))
    for t in range(count // 2):
        for tile in range(2 * width // LANES):
            span = slice(tile * LANES, (tile + 1) * LANES)
            halves = []
            for part in range(2):
                start = 16 * t + 8 * part
                quant = jnp.clip(mixed[start : start + 8, span] * inverse, -8.0, 7.0)
                root = jnp.sqrt(jnp.abs(quant)) * (CODE_TOP / math.sqrt(8.0))
                halves.append(jnp.round(jnp.where(quant < 0, -root, root)))
            code_ref[16 * t : 16 * t + 16, span] = jnp.concatenate(halves, 0).astype(I32).astype(I16)
    rest = jnp.broadcast_to(act_scale, (8, LANES)) * 4.0
    lane = iota((8, LANES), 1)
    pieces = jnp.zeros((8, LANES), F32)
    for index in range(4):
        whole = jnp.floor(rest)
        pieces = jnp.where(lane == index, whole, pieces)
        rest = (rest - whole) * 16384.0
    extra = jnp.concatenate([pieces, pieces], 0).astype(I32).astype(I16)
    for t in range(count // 2):
        code_ref[16 * t : 16 * t + 16, 2 * width :] = extra


def scale_of(pieces):
    parts = pieces.astype(I32).astype(F32)
    total = parts[:, 3:4] * 2.0**-42 + parts[:, 2:3] * 2.0**-28
    return (total + parts[:, 1:2] * 2.0**-14 + parts[:, 0:1]) * 0.25


def rotate(x, had_small):
    rows, columns = x.shape
    return pl.pallas_call(
        rotate_kernel,
        out_shape=jax.ShapeDtypeStruct((rows, columns + LANES), I16),
        in_specs=[vmem(), vmem()],
        out_specs=vmem(),
        scratch_shapes=[
            pltpu.VMEM((columns // 2, columns // 2), BF16),
            pltpu.VMEM((rows, columns), F32),
        ],
        compiler_params=params(),
        name="rotate",
    )(x, had_small)


def product_kernel(pairs, *refs):
    codes = refs[: 2 * pairs]
    w_ref = refs[2 * pairs]
    out_ref, lhs, scale = refs[-3:]
    rows = codes[0].shape[0]
    width = w_ref.shape[0]

    @pl.when((pl.program_id(0) == 0) & (pl.program_id(1) == 0))
    def _():
        for pair in range(pairs):
            for side in range(2):
                ref = codes[2 * pair + side]
                base = (2 * pair + side) * rows
                scale[base : base + rows, :] = jnp.broadcast_to(scale_of(ref[:, width:]), (rows, LANES))
                for tile in range(width // LANES):
                    span = slice(tile * LANES, (tile + 1) * LANES)
                    level = ref[:, span].astype(I32).astype(F32)
                    quant = level * jnp.abs(level) * (8.0 / CODE_TOP**2)
                    high = quant.astype(BF16)
                    low = (quant - high.astype(F32)).astype(BF16)
                    lhs[pair, side * rows : (side + 1) * rows, span] = high
                    lhs[pair, (2 + side) * rows : (3 + side) * rows, span] = low

    pair = pl.program_id(1) if pairs > 1 else 0
    both = jnp.dot(lhs[pair], w_ref[...], preferred_element_type=F32)
    start = pl.multiple_of(pair * 2 * rows, 2 * rows) if pairs > 1 else 0
    factor = scale[pl.ds(start, 2 * rows), 0:1]
    total = (both[: 2 * rows] + both[2 * rows :]) * factor
    out_ref[0] = total[:rows]
    out_ref[1] = total[rows:]


def product(codes, weight, first, held=None, block=512):
    pairs = len(codes) // 2
    rows = codes[0].shape[0]
    depth, width = weight.shape
    grid = (width // block, pairs)
    whole = pl.BlockSpec(codes[0].shape, lambda n, p: (0, 0))
    operands = list(codes) + [weight]
    in_specs = [whole] * len(codes) + [pl.BlockSpec((depth, block), lambda n, p: (0, n))]
    aliases = {}
    if held is not None:
        aliases = {len(operands): 0}
        operands.append(held)
        in_specs.append(pl.BlockSpec(memory_space=pl.ANY))
    return pl.pallas_call(
        functools.partial(product_kernel, pairs),
        grid=grid,
        out_shape=jax.ShapeDtypeStruct((8, rows, width), F32),
        in_specs=in_specs,
        out_specs=pl.BlockSpec((2, rows, block), lambda n, p: (first + p, 0, n)),
        scratch_shapes=[
            pltpu.VMEM((pairs, 4 * rows, depth), BF16),
            pltpu.VMEM((2 * pairs * rows, LANES), F32),
        ],
        input_output_aliases=aliases,
        compiler_params=params(dimension_semantics=("arbitrary", "arbitrary")),
        cost_estimate=pl.CostEstimate(
            flops=8 * pairs * rows * depth * width,
            bytes_accessed=2 * depth * width,
            transcendentals=0,
        ),
        name=f"product_{first}",
    )(*operands)


def pack(value, out_ref, index):
    width = value.shape[-1]
    top = jnp.max(jnp.abs(value), axis=-1, keepdims=True)
    level = jnp.ceil(jnp.log2(jnp.maximum(top, 1e-30)) * 256.0)
    code = jnp.round(value * (jnp.exp2(level * (-1.0 / 256.0)) * SUM_TOP))
    code = jnp.clip(code, -32767.0, 32767.0)
    if index is None:
        out_ref[:, :width] = code.astype(I32).astype(I16)
        out_ref[:, width:] = jnp.broadcast_to(level, (value.shape[0], LANES)).astype(I32).astype(I16)
    else:
        out_ref[index, :, :width] = code.astype(I32).astype(I16)
        out_ref[index, :, width:] = jnp.broadcast_to(level, (value.shape[0], LANES)).astype(I32).astype(I16)


def unpack(code):
    width = code.shape[-1] - LANES
    level = code[:, width : width + 1].astype(I32).astype(F32)
    factor = jnp.exp2(level * (1.0 / 256.0)) * (1.0 / SUM_TOP)
    return code[:, :width].astype(I32).astype(F32) * factor


def rows_at(p_ref, slot, place, part, size):
    shard = slot * 2 + (place >> 1)
    start = pl.multiple_of((place & 1) * 2 * size + part * size, size)
    return p_ref[shard, pl.ds(start, size), :]


def spread_kernel(size, at_ref, p_ref, *outs):
    for d in range(1, 4):
        for k in range(4):
            pack(rows_at(p_ref, at_ref[d], k, 0, size), outs[d - 1], k)
            pack(rows_at(p_ref, k, at_ref[4 + d], 1, size), outs[2 + d], k)


def spread(at, partial, size):
    width = partial.shape[-1]
    shape = jax.ShapeDtypeStruct((4, size, width + LANES), I16)
    return pl.pallas_call(
        functools.partial(spread_kernel, size),
        out_shape=[shape] * 6,
        in_specs=[smem(), vmem()],
        out_specs=[vmem()] * 6,
        compiler_params=params(),
        name="spread",
    )(at, partial)


def join_kernel(size, at_ref, p_ref, *refs):
    incoming = refs[:6]
    outs = refs[6:12]
    own = refs[12]
    for d in range(4):
        place = at_ref[4 + d]
        total = rows_at(p_ref, at_ref[0], place, 0, size)
        for got in incoming[:3]:
            total = total + unpack(got[place])
        if d == 0:
            own[0] = total
        else:
            pack(total, outs[d - 1], None)
        slot = at_ref[d]
        total = rows_at(p_ref, slot, at_ref[4], 1, size)
        for got in incoming[3:]:
            total = total + unpack(got[slot])
        if d == 0:
            own[1] = total
        else:
            pack(total, outs[2 + d], None)


def join(at, partial, incoming, size):
    width = partial.shape[-1]
    shape = jax.ShapeDtypeStruct((size, width + LANES), I16)
    return pl.pallas_call(
        functools.partial(join_kernel, size),
        out_shape=[shape] * 6 + [jax.ShapeDtypeStruct((2, size, width), F32)],
        in_specs=[smem()] + [vmem()] * 7,
        out_specs=[vmem()] * 7,
        compiler_params=params(),
        name="join",
    )(at, partial, *incoming)


def finish_kernel(own_ref, w_ref, *refs):
    out_ref = refs[-1]
    size = own_ref.shape[1]
    for part in range(2):
        total = own_ref[part]
        for got in refs[3 * part : 3 * part + 3]:
            total = total + unpack(got[...])
        out_ref[part * size : (part + 1) * size, :] = (total * w_ref[...]).astype(BF16)


def finish(own, w_scale, incoming):
    size, width = own.shape[1:]
    return pl.pallas_call(
        finish_kernel,
        out_shape=jax.ShapeDtypeStruct((2 * size, width), BF16),
        in_specs=[vmem()] * 8,
        out_specs=vmem(),
        compiler_params=params(),
        name="finish",
    )(own, w_scale, *incoming)


def along_x(block, apart):
    return lax.ppermute(block, "seq", [(i, (i + 2 * apart) % 8) for i in range(8)])


def other_core(block):
    return lax.ppermute(block, "seq", [(i, i ^ 1) for i in range(8)])


def along_z(block, apart):
    return lax.ppermute(block, "tensor", [(i, (i + 4 * apart) % 16) for i in range(16)])


def along_y(block, apart):
    return lax.ppermute(block, "tensor", [(i, i // 4 * 4 + (i + apart) % 4) for i in range(16)])


def local(hidden, down_int, w_scale, had_small):
    tokens, columns = hidden.shape
    ranks = lax.axis_size("tensor")
    rows = tokens // CHUNKS
    size = rows // 4
    seq, tensor = lax.axis_index("seq"), lax.axis_index("tensor")
    x, core, z, y = seq // 2, seq % 2, tensor // 4, tensor % 4
    away = jnp.arange(4, dtype=I32)
    slot = (z + away - x) % 4
    slot = jnp.where(slot == 2, 3, jnp.where(slot == 3, 2, slot))
    place = ((y + away) % 4) ^ (2 * core)
    at = jnp.concatenate([slot, place]).astype(I32)

    ordered = hidden.reshape(2, CHUNKS, rows // 2, columns).swapaxes(0, 1)
    sent = ordered.reshape(ranks, tokens // ranks, columns)
    whole = lax.all_to_all(sent, "tensor", split_axis=0, concat_axis=0, tiled=True)
    code = rotate(whole.reshape(tokens, columns), had_small)
    code = code.reshape(ranks, tokens // ranks, columns + LANES)
    back = lax.all_to_all(code, "tensor", split_axis=0, concat_axis=0, tiled=True)
    back = back.reshape(tokens, columns + LANES)
    scales = scale_of(back[:, columns : columns + LANES])[:, 0]
    act_scale = scales.reshape(CHUNKS, 2, rows // 2).swapaxes(0, 1).reshape(tokens)

    outputs = []
    for chunk in range(CHUNKS):
        own = back[chunk * rows : (chunk + 1) * rows]
        own_c = other_core(own)
        below = along_x(own, 1)
        above = along_x(own, -1)
        far = jnp.concatenate(
            [along_x(below[: rows // 2], 1), along_x(above[rows // 2 :], -1)], axis=0
        )
        above_c, below_c = other_core(above), other_core(below)
        far_c = other_core(far)
        partial = product([own, own_c], down_int, 0)
        partial = product([above, above_c, below, below_c], down_int, 1, partial)
        partial = product([far, far_c], down_int, 3, partial)
        sends = spread(at, partial, size)
        hops = (1, 2, 3)
        got = [along_z(sends[d - 1], d) for d in hops] + [along_y(sends[2 + d], d) for d in hops]
        sums = join(at, partial, got, size)
        got = [along_y(sums[d - 1], d) for d in hops] + [along_z(sums[2 + d], d) for d in hops]
        outputs.append(finish(sums[6], w_scale[None, :], got))
    mixed = outputs[0] if CHUNKS == 1 else jnp.concatenate(outputs, axis=0)
    return (mixed, act_scale)


def solution(mesh):
    return jax.shard_map(
        local,
        mesh=mesh,
        in_specs=(P("seq", "tensor"), P("tensor", "seq"), P("seq"), P()),
        out_specs=(P("tensor", "seq"), P("seq")),
        check_vma=False,
    )
```

```python
import math

import jax
import jax.numpy as jnp
from jax import lax
from jax.experimental import pallas as pl
from jax.experimental.pallas import tpu as pltpu
from jax.sharding import PartitionSpec as P

FF = 53248
HAD = 52

clip_ratio = 0.9
epsilon = 1e-05

F32, BF16, I16, I32 = jnp.float32, jnp.bfloat16, jnp.int16, jnp.int32
LANES = 128
CODE_TOP = 32767.0
SUM_TOP = 32700.0


def vmem():
    return pl.BlockSpec(memory_space=pltpu.VMEM)


def smem():
    return pl.BlockSpec(memory_space=pltpu.SMEM)


def params(mebibytes=12, **more):
    return pltpu.CompilerParams(vmem_limit_bytes=mebibytes * 1024 * 1024, **more)


def parity_sign(left, right, bits):
    both = left & right
    parity = jnp.zeros(both.shape, I32)
    for shift_bit in range(bits):
        parity = parity ^ (both >> shift_bit & 1)
    return 1 - 2 * parity


def iota(shape, dim):
    return lax.broadcasted_iota(I32, shape, dim)


def block_of(index):
    return jnp.floor((index.astype(F32) + 0.5) * (1.0 / HAD)).astype(I32)


def rotate_kernel(x_ref, had_ref, code_ref, matrix, mixed):
    width = matrix.shape[0]
    group = 4 * HAD
    row = iota((group, HAD), 0)
    pick_row = (row - HAD * block_of(row) == iota((group, HAD), 1)).astype(BF16)
    lane = iota((HAD, width), 1)
    pick_lane = (lane - HAD * block_of(lane) == iota((HAD, width), 0)).astype(BF16)
    small = had_ref[...].astype(F32).astype(BF16)
    tiled = jnp.dot(small, pick_lane, preferred_element_type=F32).astype(BF16)
    base = jnp.dot(pick_row, tiled, preferred_element_type=F32)
    row_block = block_of(iota((group, width), 0))
    lane_block = block_of(iota((group, width), 1))
    base = base * parity_sign(row_block, lane_block & 3, 2).astype(F32)
    line_block = block_of(iota((8, width), 1)) >> 2
    lines = parity_sign(iota((8, width), 0), line_block, 3).astype(F32)
    for g in range(width // group):
        matrix[g * group : (g + 1) * group, :] = (base * lines[g : g + 1, :]).astype(BF16)
    rows = x_ref.shape[0]
    count = rows // 8
    for half in range(2):
        span = slice(half * width, (half + 1) * width)
        mixed[:, span] = jnp.dot(x_ref[:, span], matrix[...], preferred_element_type=F32)
    norm_factor = jnp.float32(1.0 / math.sqrt(FF))
    top = jnp.zeros((8, LANES), F32)
    for tile in range(width // LANES):
        columns = [slice(half * width + tile * LANES, half * width + (tile + 1) * LANES) for half in range(2)]
        values = [mixed[8 * t : 8 * t + 8, span] for span in columns for t in range(count)]
        step = 1
        while step < len(values):
            for low in range(len(values)):
                if not low & step:
                    a, b = values[low], values[low | step]
                    values[low], values[low | step] = a + b, a - b
            step *= 2
        for index, value in enumerate(values):
            half, t = index // count, index % count
            value = value * norm_factor
            top = jnp.maximum(top, jnp.abs(value))
            mixed[8 * t : 8 * t + 8, columns[half]] = value
    peak = jnp.max(top, axis=1, keepdims=True)
    act_scale = clip_ratio / 7.0 * (peak + epsilon)
    inverse = jnp.broadcast_to(1.0 / act_scale, (8, LANES))
    for t in range(count // 2):
        for tile in range(2 * width // LANES):
            span = slice(tile * LANES, (tile + 1) * LANES)
            halves = []
            for part in range(2):
                start = 16 * t + 8 * part
                quant = jnp.clip(mixed[start : start + 8, span] * inverse, -8.0, 7.0)
                root = jnp.sqrt(jnp.abs(quant)) * (CODE_TOP / math.sqrt(8.0))
                halves.append(jnp.round(jnp.where(quant < 0, -root, root)))
            code_ref[16 * t : 16 * t + 16, span] = jnp.concatenate(halves, 0).astype(I32).astype(I16)
    rest = jnp.broadcast_to(act_scale, (8, LANES)) * 4.0
    lane = iota((8, LANES), 1)
    pieces = jnp.zeros((8, LANES), F32)
    for index in range(4):
        whole = jnp.floor(rest)
        pieces = jnp.where(lane == index, whole, pieces)
        rest = (rest - whole) * 16384.0
    extra = jnp.concatenate([pieces, pieces], 0).astype(I32).astype(I16)
    for t in range(count // 2):
        code_ref[16 * t : 16 * t + 16, 2 * width :] = extra


def scale_of(pieces):
    parts = pieces.astype(I32).astype(F32)
    total = parts[:, 3:4] * 2.0**-42 + parts[:, 2:3] * 2.0**-28
    return (total + parts[:, 1:2] * 2.0**-14 + parts[:, 0:1]) * 0.25


def rotate(x, had_small):
    rows, columns = x.shape
    return pl.pallas_call(
        rotate_kernel,
        out_shape=jax.ShapeDtypeStruct((rows, columns + LANES), I16),
        in_specs=[vmem(), vmem()],
        out_specs=vmem(),
        scratch_shapes=[
            pltpu.VMEM((columns // 2, columns // 2), BF16),
            pltpu.VMEM((rows, columns), F32),
        ],
        compiler_params=params(24),
        name="rotate",
    )(x, had_small)


def product_kernel(at_ref, own_ref, other_ref, w_ref, *refs):
    sends, kept, lhs, total, scale = refs[:3], refs[3], refs[4], refs[5], refs[6]
    rows = own_ref.shape[0]
    size = kept.shape[0]
    depth = w_ref.shape[0]
    block = w_ref.shape[1]
    step = pl.program_id(0)

    @pl.when(step == 0)
    def _():
        for side, ref in enumerate((own_ref, other_ref)):
            base = side * rows
            scale[base : base + rows, :] = jnp.broadcast_to(scale_of(ref[:, depth:]), (rows, LANES))
            for tile in range(depth // LANES):
                span = slice(tile * LANES, (tile + 1) * LANES)
                level = ref[:, span].astype(I32).astype(F32)
                quant = level * jnp.abs(level) * (8.0 / CODE_TOP**2)
                high = quant.astype(BF16)
                low = (quant - high.astype(F32)).astype(BF16)
                lhs[base : base + rows, span] = high
                lhs[2 * rows + base : 2 * rows + base + rows, span] = low

    both = jnp.dot(lhs[...], w_ref[...], preferred_element_type=F32)
    start = pl.multiple_of(step * block, block)
    total[:, pl.ds(start, block)] = (both[: 2 * rows] + both[2 * rows :]) * scale[:, 0:1]

    @pl.when(step == pl.num_programs(0) - 1)
    def _():
        for d in range(4):
            first = pl.multiple_of(at_ref[4 + d] * size, size)
            value = total[pl.ds(first, size), :]
            if d == 0:
                kept[...] = value
            else:
                pack(value, sends[d - 1])


def product(at, own, other, weight, name, block=512):
    rows = own.shape[0]
    size = rows // 2
    depth, width = weight.shape
    whole = pl.BlockSpec(own.shape, lambda n: (0, 0))
    message = jax.ShapeDtypeStruct((size, width + LANES), I16)
    return pl.pallas_call(
        product_kernel,
        grid=(width // block,),
        out_shape=[message] * 3 + [jax.ShapeDtypeStruct((size, width), F32)],
        in_specs=[smem(), whole, whole, pl.BlockSpec((depth, block), lambda n: (0, n))],
        out_specs=[pl.BlockSpec(message.shape, lambda n: (0, 0))] * 3
        + [pl.BlockSpec((size, width), lambda n: (0, 0))],
        scratch_shapes=[
            pltpu.VMEM((4 * rows, depth), BF16),
            pltpu.VMEM((2 * rows, width), F32),
            pltpu.VMEM((2 * rows, LANES), F32),
        ],
        compiler_params=params(26, dimension_semantics=("arbitrary",)),
        cost_estimate=pl.CostEstimate(
            flops=8 * rows * depth * width,
            bytes_accessed=2 * depth * width,
            transcendentals=0,
        ),
        name=name,
    )(at, own, other, weight)


def pack(value, out_ref):
    width = value.shape[-1]
    top = jnp.max(jnp.abs(value), axis=-1, keepdims=True)
    level = jnp.ceil(jnp.log2(jnp.maximum(top, 1e-30)) * 256.0)
    code = jnp.round(value * (jnp.exp2(level * (-1.0 / 256.0)) * SUM_TOP))
    code = jnp.clip(code, -32767.0, 32767.0)
    out_ref[:, :width] = code.astype(I32).astype(I16)
    out_ref[:, width:] = jnp.broadcast_to(level, (value.shape[0], LANES)).astype(I32).astype(I16)


def unpack(code):
    width = code.shape[-1] - LANES
    level = code[:, width : width + 1].astype(I32).astype(F32)
    factor = jnp.exp2(level * (1.0 / 256.0)) * (1.0 / SUM_TOP)
    return code[:, :width].astype(I32).astype(F32) * factor


def join_kernel(kept, a, b, c, out_ref):
    out_ref[...] = kept[...] + unpack(a[...]) + unpack(b[...]) + unpack(c[...])


def join(kept, got, name):
    return pl.pallas_call(
        join_kernel,
        out_shape=jax.ShapeDtypeStruct(kept.shape, F32),
        in_specs=[vmem()] * 4,
        out_specs=vmem(),
        compiler_params=params(),
        name=name,
    )(kept, *got)


def collect_kernel(at_ref, first, second, third, kept, a, b, c, *refs):
    sends, own_ref, held = refs[:3], refs[3], refs[4]
    held[0] = first[...]
    held[1] = second[...]
    held[2] = third[...]
    held[3] = kept[...] + unpack(a[...]) + unpack(b[...]) + unpack(c[...])
    for d in range(4):
        value = held[at_ref[d]]
        if d == 0:
            own_ref[...] = value
        else:
            pack(value, sends[d - 1])


def collect(at, sums, kept, got):
    size, width = kept.shape
    message = jax.ShapeDtypeStruct((size, width + LANES), I16)
    return pl.pallas_call(
        collect_kernel,
        out_shape=[message] * 3 + [jax.ShapeDtypeStruct(kept.shape, F32)],
        in_specs=[smem()] + [vmem()] * 7,
        out_specs=[vmem()] * 4,
        scratch_shapes=[pltpu.VMEM((4, size, width), F32)],
        compiler_params=params(),
        name="collect",
    )(at, *sums, kept, *got)


def finish_kernel(own_ref, w_ref, a, b, c, out_ref):
    total = own_ref[...] + unpack(a[...]) + unpack(b[...]) + unpack(c[...])
    out_ref[...] = (total * w_ref[...]).astype(BF16)


def finish(own, w_scale, got):
    return pl.pallas_call(
        finish_kernel,
        out_shape=jax.ShapeDtypeStruct(own.shape, BF16),
        in_specs=[vmem()] * 5,
        out_specs=vmem(),
        compiler_params=params(),
        name="finish",
    )(own, w_scale, *got)


def along_x(block, apart):
    return lax.ppermute(block, "seq", [(i, (i + 2 * apart) % 8) for i in range(8)])


def other_core(block):
    return lax.ppermute(block, "seq", [(i, i ^ 1) for i in range(8)])


def along_z(blocks):
    return [
        lax.ppermute(block, "tensor", [(i, (i + 4 * apart) % 16) for i in range(16)])
        for apart, block in enumerate(blocks, 1)
    ]


def along_y(blocks):
    return [
        lax.ppermute(block, "tensor", [(i, i // 4 * 4 + (i + apart) % 4) for i in range(16)])
        for apart, block in enumerate(blocks, 1)
    ]


def local(hidden, down_int, w_scale, had_small):
    tokens, columns = hidden.shape
    ranks = lax.axis_size("tensor")
    half = tokens // 2
    seq, tensor = lax.axis_index("seq"), lax.axis_index("tensor")
    x, core, z, y = seq // 2, seq % 2, tensor // 4, tensor % 4
    away = jnp.arange(4, dtype=I32)
    slot = (z + away - x) % 4
    slot = jnp.where(slot == 2, 3, jnp.where(slot == 3, 2, slot))
    place = ((y + away) % 4) ^ (2 * core)
    at = jnp.concatenate([slot, place]).astype(I32)
    at, hidden = lax.optimization_barrier((at, hidden))

    sent = hidden.reshape(ranks, tokens // ranks, columns)
    whole = lax.all_to_all(sent, "tensor", split_axis=0, concat_axis=0, tiled=True)
    code = rotate(whole.reshape(tokens, columns), had_small)
    code = code.reshape(ranks, tokens // ranks, columns + LANES)
    back = lax.all_to_all(code, "tensor", split_axis=0, concat_axis=0, tiled=True)
    own = back.reshape(tokens, columns + LANES)
    act_scale = scale_of(own[:, columns : columns + LANES])[:, 0]

    own_c = other_core(own)
    below = along_x(own, 1)
    above = along_x(own, -1)
    *sends, kept_0 = product(at, own, own_c, down_int, "product_0")
    sends, below, above = lax.optimization_barrier((sends, below, above))
    got_0 = along_y(sends)
    above_c, below_c = other_core(above), other_core(below)
    far = [along_x(below[:half], 1), along_x(above[half:], -1)]
    *sends, kept_1 = product(at, above, above_c, down_int, "product_1")
    sends, far, got_0, below = lax.optimization_barrier((sends, far, got_0, below))
    got_1 = along_y(sends)
    far = jnp.concatenate(far, axis=0)
    far_c = other_core(far)
    sum_0 = join(kept_0, got_0, "join_0")
    below, sum_0 = lax.optimization_barrier((below, sum_0))
    *sends, kept_2 = product(at, below, below_c, down_int, "product_2")
    sends, far, far_c, got_1 = lax.optimization_barrier((sends, far, far_c, got_1))
    got_2 = along_y(sends)
    sum_1 = join(kept_1, got_1, "join_1")
    far, sum_1 = lax.optimization_barrier((far, sum_1))
    *sends, kept_3 = product(at, far, far_c, down_int, "product_3")
    sends, got_2 = lax.optimization_barrier((sends, got_2))
    got_3 = along_y(sends)
    sum_2 = join(kept_2, got_2, "join_2")
    *sends, own_sum = collect(at, [sum_0, sum_1, sum_2], kept_3, got_3)
    mixed = finish(own_sum, w_scale[None, :], along_z(sends))
    return (mixed, act_scale)


def solution(mesh):
    return jax.shard_map(
        local,
        mesh=mesh,
        in_specs=(P("seq", "tensor"), P("tensor", "seq"), P("seq"), P()),
        out_specs=(P("tensor", "seq"), P("seq")),
        check_vma=False,
    )
```

```python
import functools
import math

import jax
import jax.numpy as jnp
from jax import lax
from jax.experimental import pallas as pl
from jax.experimental.pallas import tpu as pltpu
from jax.sharding import PartitionSpec as P

FF = 53248
HAD = 52

clip_ratio = 0.9
epsilon = 1e-05

F32, BF16, I16, I32 = jnp.float32, jnp.bfloat16, jnp.int16, jnp.int32
LANES = 128
CODE_TOP = 32767.0
SUM_TOP = 32700.0
BLOCK = 512


def vmem():
    return pl.BlockSpec(memory_space=pltpu.VMEM)


def smem():
    return pl.BlockSpec(memory_space=pltpu.SMEM)


def params(mebibytes=12, **more):
    return pltpu.CompilerParams(vmem_limit_bytes=mebibytes * 1024 * 1024, **more)


def parity_sign(left, right, bits):
    both = left & right
    parity = jnp.zeros(both.shape, I32)
    for shift_bit in range(bits):
        parity = parity ^ (both >> shift_bit & 1)
    return 1 - 2 * parity


def iota(shape, dim):
    return lax.broadcasted_iota(I32, shape, dim)


def block_of(index):
    return jnp.floor((index.astype(F32) + 0.5) * (1.0 / HAD)).astype(I32)


def rotate_kernel(x_ref, had_ref, w_ref, code_ref, held_ref, matrix, mixed, sem):
    fetch = pltpu.make_async_copy(w_ref, held_ref, sem)
    fetch.start()
    width = matrix.shape[0]
    group = 4 * HAD
    row = iota((group, HAD), 0)
    pick_row = (row - HAD * block_of(row) == iota((group, HAD), 1)).astype(BF16)
    lane = iota((HAD, width), 1)
    pick_lane = (lane - HAD * block_of(lane) == iota((HAD, width), 0)).astype(BF16)
    small = had_ref[...].astype(F32).astype(BF16)
    tiled = jnp.dot(small, pick_lane, preferred_element_type=F32).astype(BF16)
    base = jnp.dot(pick_row, tiled, preferred_element_type=F32)
    row_block = block_of(iota((group, width), 0))
    lane_block = block_of(iota((group, width), 1))
    base = base * parity_sign(row_block, lane_block & 3, 2).astype(F32)
    line_block = block_of(iota((8, width), 1)) >> 2
    lines = parity_sign(iota((8, width), 0), line_block, 3).astype(F32)
    for g in range(width // group):
        matrix[g * group : (g + 1) * group, :] = (base * lines[g : g + 1, :]).astype(BF16)
    rows = x_ref.shape[0]
    count = rows // 8
    for half in range(2):
        span = slice(half * width, (half + 1) * width)
        mixed[:, span] = jnp.dot(x_ref[:, span], matrix[...], preferred_element_type=F32)
    norm_factor = jnp.float32(1.0 / math.sqrt(FF))
    top = jnp.zeros((8, LANES), F32)
    for tile in range(width // LANES):
        columns = [slice(half * width + tile * LANES, half * width + (tile + 1) * LANES) for half in range(2)]
        values = [mixed[8 * t : 8 * t + 8, span] for span in columns for t in range(count)]
        step = 1
        while step < len(values):
            for low in range(len(values)):
                if not low & step:
                    a, b = values[low], values[low | step]
                    values[low], values[low | step] = a + b, a - b
            step *= 2
        for index, value in enumerate(values):
            half, t = index // count, index % count
            value = value * norm_factor
            top = jnp.maximum(top, jnp.abs(value))
            mixed[8 * t : 8 * t + 8, columns[half]] = value
    peak = jnp.max(top, axis=1, keepdims=True)
    act_scale = clip_ratio / 7.0 * (peak + epsilon)
    inverse = jnp.broadcast_to(1.0 / act_scale, (8, LANES))
    for t in range(count // 2):
        for tile in range(2 * width // LANES):
            span = slice(tile * LANES, (tile + 1) * LANES)
            halves = []
            for part in range(2):
                start = 16 * t + 8 * part
                quant = jnp.clip(mixed[start : start + 8, span] * inverse, -8.0, 7.0)
                root = jnp.sqrt(jnp.abs(quant)) * (CODE_TOP / math.sqrt(8.0))
                halves.append(jnp.round(jnp.where(quant < 0, -root, root)))
            code_ref[16 * t : 16 * t + 16, span] = jnp.concatenate(halves, 0).astype(I32).astype(I16)
    rest = jnp.broadcast_to(act_scale, (8, LANES)) * 4.0
    lane = iota((8, LANES), 1)
    pieces = jnp.zeros((8, LANES), F32)
    for index in range(4):
        whole = jnp.floor(rest)
        pieces = jnp.where(lane == index, whole, pieces)
        rest = (rest - whole) * 16384.0
    extra = jnp.concatenate([pieces, pieces], 0).astype(I32).astype(I16)
    for t in range(count // 2):
        code_ref[16 * t : 16 * t + 16, 2 * width :] = extra
    fetch.wait()


def scale_of(pieces):
    parts = pieces.astype(I32).astype(F32)
    total = parts[:, 3:4] * 2.0**-42 + parts[:, 2:3] * 2.0**-28
    return (total + parts[:, 1:2] * 2.0**-14 + parts[:, 0:1]) * 0.25


def rotate(x, had_small, weight):
    rows, columns = x.shape
    return pl.pallas_call(
        rotate_kernel,
        out_shape=[
            jax.ShapeDtypeStruct((rows, columns + LANES), I16),
            jax.ShapeDtypeStruct(weight.shape, weight.dtype),
        ],
        in_specs=[vmem(), vmem(), pl.BlockSpec(memory_space=pltpu.HBM)],
        out_specs=[vmem(), vmem()],
        scratch_shapes=[
            pltpu.VMEM((columns // 2, columns // 2), BF16),
            pltpu.VMEM((rows, columns), F32),
            pltpu.SemaphoreType.DMA,
        ],
        compiler_params=params(34),
        name="rotate",
    )(x, had_small, weight)


def product_kernel(at_ref, *refs):
    codes, w_ref = refs[:4], refs[4]
    sends, kept, lhs, total, scale = refs[5:8], refs[8], refs[9], refs[10], refs[11]
    rows = scale.shape[0] // 4
    size = rows // 2
    depth, width = w_ref.shape
    for index, ref in enumerate(codes):
        base = index * rows
        scale[base : base + rows, :] = jnp.broadcast_to(scale_of(ref[:, depth:]), (rows, LANES))
        for tile in range(depth // LANES):
            span = slice(tile * LANES, (tile + 1) * LANES)
            level = ref[:, span].astype(I32).astype(F32)
            quant = level * jnp.abs(level) * (8.0 / CODE_TOP**2)
            high = quant.astype(BF16)
            low = (quant - high.astype(F32)).astype(BF16)
            lhs[base : base + rows, span] = high
            lhs[4 * rows + base : 4 * rows + base + rows, span] = low

    def columns(step, carry):
        start = pl.multiple_of(step * BLOCK, BLOCK)
        both = jnp.dot(lhs[...], w_ref[:, pl.ds(start, BLOCK)], preferred_element_type=F32)
        total[:, pl.ds(start, BLOCK)] = (both[: 4 * rows] + both[4 * rows :]) * scale[:, 0:1]
        return carry

    lax.fori_loop(0, width // BLOCK, columns, 0)
    for d in range(4):
        for group in range(2):
            first = pl.multiple_of(group * 2 * rows + at_ref[4 + d] * size, size)
            value = total[pl.ds(first, size), :]
            span = slice(group * size, (group + 1) * size)
            if d == 0:
                kept[span, :] = value
            else:
                pack(value, sends[d - 1], span)


def product(at, codes, weight):
    rows = codes[0][0].shape[0] if codes[0][1] is None else codes[0][0].shape[0] // 2
    depth, width = weight.shape
    message = jax.ShapeDtypeStruct((rows, width + LANES), I16)
    specs = [
        pl.BlockSpec((rows, depth + LANES), functools.partial(lambda index, n: (index, 0), index or 0))
        for _, index in codes
    ]
    return pl.pallas_call(
        product_kernel,
        grid=(1,),
        out_shape=[message] * 3 + [jax.ShapeDtypeStruct((rows, width), F32)],
        in_specs=[smem()] + specs + [vmem()],
        out_specs=[pl.BlockSpec(message.shape, lambda n: (0, 0))] * 3
        + [pl.BlockSpec((rows, width), lambda n: (0, 0))],
        scratch_shapes=[
            pltpu.VMEM((8 * rows, depth), BF16),
            pltpu.VMEM((4 * rows, width), F32),
            pltpu.VMEM((4 * rows, LANES), F32),
        ],
        compiler_params=params(26),
        cost_estimate=pl.CostEstimate(
            flops=16 * rows * depth * width,
            bytes_accessed=2 * depth * width,
            transcendentals=0,
        ),
    )(at, *[array for array, _ in codes], weight)


def pack(value, out_ref, span=slice(None)):
    width = value.shape[-1]
    top = jnp.max(jnp.abs(value), axis=-1, keepdims=True)
    level = jnp.ceil(jnp.log2(jnp.maximum(top, 1e-30)) * 256.0)
    code = jnp.round(value * (jnp.exp2(level * (-1.0 / 256.0)) * SUM_TOP))
    code = jnp.clip(code, -32767.0, 32767.0)
    out_ref[span, :width] = code.astype(I32).astype(I16)
    out_ref[span, width:] = jnp.broadcast_to(level, (value.shape[0], LANES)).astype(I32).astype(I16)


def unpack(code):
    width = code.shape[-1] - LANES
    level = code[:, width : width + 1].astype(I32).astype(F32)
    factor = jnp.exp2(level * (1.0 / 256.0)) * (1.0 / SUM_TOP)
    return code[:, :width].astype(I32).astype(F32) * factor


def collect_kernel(at_ref, *refs):
    sends, own_ref, held = refs[16:19], refs[19], refs[20]
    half = own_ref.shape[0] // 2
    for chunk in range(4):
        kept, a, b, c = refs[4 * chunk : 4 * chunk + 4]
        value = kept[...] + unpack(a[...]) + unpack(b[...]) + unpack(c[...])
        for group in range(2):
            if chunk in (0, 3):
                held[chunk, group * half : (group + 1) * half, :] = value[group * half : (group + 1) * half]
            else:
                held[1 + group, (chunk - 1) * half : chunk * half, :] = value[group * half : (group + 1) * half]
    for d in range(4):
        value = held[at_ref[d]]
        if d == 0:
            own_ref[...] = value
        else:
            pack(value, sends[d - 1])


def collect(at, parts):
    size, width = parts[0].shape
    message = jax.ShapeDtypeStruct((size, width + LANES), I16)
    return pl.pallas_call(
        collect_kernel,
        out_shape=[message] * 3 + [jax.ShapeDtypeStruct((size, width), F32)],
        in_specs=[smem()] + [vmem()] * 16,
        out_specs=[vmem()] * 4,
        scratch_shapes=[pltpu.VMEM((4, size, width), F32)],
        compiler_params=params(16),
        name="collect",
    )(at, *parts)


def finish_kernel(own_ref, w_ref, a, b, c, out_ref):
    total = own_ref[...] + unpack(a[...]) + unpack(b[...]) + unpack(c[...])
    out_ref[...] = (total * w_ref[...]).astype(BF16)


def finish(own, w_scale, got):
    return pl.pallas_call(
        finish_kernel,
        out_shape=jax.ShapeDtypeStruct(own.shape, BF16),
        in_specs=[vmem()] * 5,
        out_specs=vmem(),
        compiler_params=params(),
        name="finish",
    )(own, w_scale, *got)


def along_x(block, apart):
    return lax.ppermute(block, "seq", [(i, (i + 2 * apart) % 8) for i in range(8)])


def other_core(block):
    return lax.ppermute(block, "seq", [(i, i ^ 1) for i in range(8)])


def along_z(blocks):
    return [
        lax.ppermute(block, "tensor", [(i, (i + 4 * apart) % 16) for i in range(16)])
        for apart, block in enumerate(blocks, 1)
    ]


def along_y(blocks):
    got = []
    for apart, block in enumerate(blocks, 1):
        route = [(i, i // 4 * 4 + (i + apart) % 4) for i in range(16)]
        got.append(lax.ppermute(block, "tensor", route))
    return got


def step(hidden, down_int, w_scale, had_small):
    tokens, columns = hidden.shape
    ranks = lax.axis_size("tensor")
    half, quarter = tokens // 2, tokens // 4
    seq, tensor = lax.axis_index("seq"), lax.axis_index("tensor")
    x, core, z, y = seq // 2, seq % 2, tensor // 4, tensor % 4
    away = jnp.arange(4, dtype=I32)
    slot = (z + away - x) % 4
    slot = jnp.where(slot == 2, 3, jnp.where(slot == 3, 2, slot))
    place = ((y + away) % 4) ^ (2 * core)
    at = jnp.concatenate([slot, place]).astype(I32)
    at, hidden = lax.optimization_barrier((at, hidden))

    ordered = hidden.reshape(2, 2, quarter, columns).swapaxes(0, 1)
    sent = ordered.reshape(ranks, tokens // ranks, columns)
    whole = lax.all_to_all(sent, "tensor", split_axis=0, concat_axis=0, tiled=True)
    code, weight = rotate(whole.reshape(tokens, columns), had_small, down_int)
    code = code.reshape(ranks, tokens // ranks, columns + LANES)
    back = lax.all_to_all(code, "tensor", split_axis=0, concat_axis=0, tiled=True)
    own = back.reshape(tokens, columns + LANES)
    scales = scale_of(own[:, columns : columns + LANES])[:, 0]
    act_scale = scales.reshape(2, 2, quarter).swapaxes(0, 1).reshape(tokens)

    own_c = other_core(own)
    below_0, above_0 = along_x(own[:half], 1), along_x(own[:half], -1)
    below_1, above_1 = along_x(own[half:], 1), along_x(own[half:], -1)
    codes = [(own, 0), (own_c, 0), (own, 1), (own_c, 1)]
    *sends, kept_0 = product(at, codes, weight)
    sends, below_0, above_0 = lax.optimization_barrier((sends, below_0, above_0))
    got_0 = along_y(sends)
    far_0 = along_x(below_0, 1)
    codes = [above_0, other_core(above_0), below_0, other_core(below_0)]
    *sends, kept_1 = product(at, [(code, None) for code in codes], weight)
    sends, below_1, above_1 = lax.optimization_barrier((sends, below_1, above_1))
    got_1 = along_y(sends)
    far_1 = along_x(above_1, -1)
    codes = [above_1, other_core(above_1), below_1, other_core(below_1)]
    *sends, kept_2 = product(at, [(code, None) for code in codes], weight)
    sends, far_0, far_1 = lax.optimization_barrier((sends, far_0, far_1))
    got_2 = along_y(sends)
    codes = [far_0, other_core(far_0), far_1, other_core(far_1)]
    *sends, kept_3 = product(at, [(code, None) for code in codes], weight)
    got_3 = along_y(sends)
    parts = [kept_0, *got_0, kept_1, *got_1, kept_2, *got_2, kept_3, *got_3]
    *sends, own_sum = collect(at, parts)
    mixed = finish(own_sum, w_scale[None, :], along_z(sends))
    return (mixed, act_scale)


def solution(mesh):
    return jax.shard_map(
        step,
        mesh=mesh,
        in_specs=(P("seq", "tensor"), P("tensor", "seq"), P("seq"), P()),
        out_specs=(P("tensor", "seq"), P("seq")),
        check_vma=False,
    )
```

```python
import functools
import math

import jax
import jax.numpy as jnp
from jax import lax
from jax.experimental import pallas as pl
from jax.experimental.pallas import tpu as pltpu
from jax.sharding import PartitionSpec as P

FF = 53248
HAD = 52

clip_ratio = 0.9
epsilon = 1e-05

F32, BF16, I16, I32 = jnp.float32, jnp.bfloat16, jnp.int16, jnp.int32
LANES = 128
CODE_TOP = 32767.0
SUM_TOP = 32700.0
BLOCK = 512
ROWS = 64


def vmem():
    return pl.BlockSpec(memory_space=pltpu.VMEM)


def params(mebibytes=12, **more):
    return pltpu.CompilerParams(vmem_limit_bytes=mebibytes * 1024 * 1024, **more)


def slot_of(apart):
    ahead = ((lax.axis_index("tensor") >> 2) + apart - (lax.axis_index("seq") >> 1)) & 3
    return ahead ^ (ahead >> 1)


def place_of(apart):
    return ((lax.axis_index("tensor") + apart) & 3) ^ ((lax.axis_index("seq") & 1) * 2)


def parity_sign(left, right, bits):
    both = left & right
    parity = jnp.zeros(both.shape, I32)
    for shift_bit in range(bits):
        parity = parity ^ (both >> shift_bit & 1)
    return 1 - 2 * parity


def iota(shape, dim):
    return lax.broadcasted_iota(I32, shape, dim)


def block_of(index):
    return jnp.floor((index.astype(F32) + 0.5) * (1.0 / HAD)).astype(I32)


def rotate_kernel(x_ref, had_ref, w_ref, code_ref, held_ref, matrix, mixed, sem):
    fetch = pltpu.make_async_copy(w_ref, held_ref, sem)
    fetch.start()
    width = matrix.shape[0]
    group = 4 * HAD
    row = iota((group, HAD), 0)
    pick_row = (row - HAD * block_of(row) == iota((group, HAD), 1)).astype(BF16)
    lane = iota((HAD, width), 1)
    pick_lane = (lane - HAD * block_of(lane) == iota((HAD, width), 0)).astype(BF16)
    small = had_ref[...]
    tiled = jnp.dot(small, pick_lane, preferred_element_type=F32).astype(BF16)
    base = jnp.dot(pick_row, tiled, preferred_element_type=F32)
    row_block = block_of(iota((group, width), 0))
    lane_block = block_of(iota((group, width), 1))
    base = base * parity_sign(row_block, lane_block & 3, 2).astype(F32)
    line_block = block_of(iota((8, width), 1)) >> 2
    lines = parity_sign(iota((8, width), 0), line_block, 3).astype(F32)
    for g in range(width // group):
        matrix[g * group : (g + 1) * group, :] = (base * lines[g : g + 1, :]).astype(BF16)
    rows = x_ref.shape[0]
    count = rows // 8
    for half in range(2):
        span = slice(half * width, (half + 1) * width)
        mixed[:, span] = jnp.dot(x_ref[:, span], matrix[...], preferred_element_type=F32)
    norm_factor = jnp.float32(1.0 / math.sqrt(FF))
    top = jnp.zeros((8, LANES), F32)
    for tile in range(width // LANES):
        columns = [slice(half * width + tile * LANES, half * width + (tile + 1) * LANES) for half in range(2)]
        values = [mixed[8 * t : 8 * t + 8, span] for span in columns for t in range(count)]
        step = 1
        while step < len(values):
            for low in range(len(values)):
                if not low & step:
                    a, b = values[low], values[low | step]
                    values[low], values[low | step] = a + b, a - b
            step *= 2
        for index, value in enumerate(values):
            half, t = index // count, index % count
            value = value * norm_factor
            top = jnp.maximum(top, jnp.abs(value))
            mixed[8 * t : 8 * t + 8, columns[half]] = value
    peak = jnp.max(top, axis=1, keepdims=True)
    act_scale = clip_ratio / 7.0 * (peak + epsilon)
    inverse = jnp.broadcast_to(1.0 / act_scale, (8, LANES))
    for t in range(count // 2):
        for tile in range(2 * width // LANES):
            span = slice(tile * LANES, (tile + 1) * LANES)
            halves = []
            for part in range(2):
                start = 16 * t + 8 * part
                quant = jnp.clip(mixed[start : start + 8, span] * inverse, -8.0, 7.0)
                root = jnp.sqrt(jnp.abs(quant)) * (CODE_TOP / math.sqrt(8.0))
                halves.append(jnp.round(jnp.where(quant < 0, -root, root)))
            code_ref[16 * t : 16 * t + 16, span] = jnp.concatenate(halves, 0).astype(I32).astype(I16)
    rest = jnp.broadcast_to(act_scale, (8, LANES)) * 4.0
    lane = iota((8, LANES), 1)
    pieces = jnp.zeros((8, LANES), F32)
    for index in range(4):
        whole = jnp.floor(rest)
        pieces = jnp.where(lane == index, whole, pieces)
        rest = (rest - whole) * 16384.0
    extra = jnp.concatenate([pieces, pieces], 0).astype(I32).astype(I16)
    for t in range(count // 2):
        code_ref[16 * t : 16 * t + 16, 2 * width :] = extra
    fetch.wait()


def scale_of(pieces):
    parts = pieces.astype(I32).astype(F32)
    total = parts[:, 3:4] * 2.0**-42 + parts[:, 2:3] * 2.0**-28
    return (total + parts[:, 1:2] * 2.0**-14 + parts[:, 0:1]) * 0.25


def rotate(x, had_small, weight):
    rows, columns = x.shape
    return pl.pallas_call(
        rotate_kernel,
        out_shape=[
            jax.ShapeDtypeStruct((rows, columns + LANES), I16),
            jax.ShapeDtypeStruct(weight.shape, weight.dtype),
        ],
        in_specs=[vmem(), vmem(), pl.BlockSpec(memory_space=pltpu.HBM)],
        out_specs=[vmem(), vmem()],
        scratch_shapes=[
            pltpu.VMEM((columns // 2, columns // 2), BF16),
            pltpu.VMEM((rows, columns), F32),
            pltpu.SemaphoreType.DMA,
        ],
        compiler_params=params(34),
        name="rotate",
    )(x, had_small, weight)


def product_kernel(strides, parts, *refs):
    codes, w_ref = refs[:4], refs[4]
    outs, (lhs, total, scale) = refs[5:-3], refs[-3:]
    rows = scale.shape[0] // 4
    size = rows // 2
    depth, width = w_ref.shape
    for index, ref in enumerate(codes):
        base = index * rows
        scale[base : base + rows, :] = jnp.broadcast_to(scale_of(ref[:, depth:]), (rows, LANES))
        for tile in range(depth // LANES):
            span = slice(tile * LANES, (tile + 1) * LANES)
            level = ref[:, span].astype(I32).astype(F32)
            quant = level * jnp.abs(level) * (8.0 / CODE_TOP**2)
            high = quant.astype(BF16)
            low = (quant - high.astype(F32)).astype(BF16)
            lhs[base : base + rows, span] = high
            lhs[4 * rows + base : 4 * rows + base + rows, span] = low

    def columns(step, carry):
        start = pl.multiple_of(step * BLOCK, BLOCK)
        both = jnp.dot(lhs[...], w_ref[:, pl.ds(start, BLOCK)], preferred_element_type=F32)
        total[:, pl.ds(start, BLOCK)] = (both[: 4 * rows] + both[4 * rows :]) * scale[:, 0:1]
        return carry

    lax.fori_loop(0, width // BLOCK, columns, 0)
    for group in range(2):
        chosen = outs if parts == 1 else outs[4 * group : 4 * group + 4]
        span = slice(group * size, (group + 1) * size) if parts == 1 else slice(None)
        for d in range(4):
            first = pl.multiple_of(group * strides[0] + place_of(d) * strides[1], size)
            value = total[pl.ds(first, size), :]
            if d == 0:
                chosen[3][span, :] = value
            else:
                pack(value, chosen[d - 1], span)


def product(codes, weight, strides, parts=1):
    rows = ROWS
    depth, width = weight.shape
    size = rows // parts
    outs = [jax.ShapeDtypeStruct((size, width + LANES), I16)] * 3 + [jax.ShapeDtypeStruct((size, width), F32)]
    outs = outs * parts
    specs = [
        pl.BlockSpec((rows, depth + LANES), functools.partial(lambda index, n: (index, 0), index))
        for _, index in codes
    ]
    return pl.pallas_call(
        functools.partial(product_kernel, strides, parts),
        grid=(1,),
        out_shape=outs,
        in_specs=specs + [vmem()],
        out_specs=[pl.BlockSpec(out.shape, lambda n: (0, 0)) for out in outs],
        scratch_shapes=[
            pltpu.VMEM((8 * rows, depth), BF16),
            pltpu.VMEM((4 * rows, width), F32),
            pltpu.VMEM((4 * rows, LANES), F32),
        ],
        compiler_params=params(26),
        cost_estimate=pl.CostEstimate(
            flops=16 * rows * depth * width,
            bytes_accessed=2 * depth * width,
            transcendentals=0,
        ),
    )(*[array for array, _ in codes], weight)


def pack(value, out_ref, span=slice(None)):
    width = value.shape[-1]
    top = jnp.max(jnp.abs(value), axis=-1, keepdims=True)
    level = jnp.ceil(jnp.log2(jnp.maximum(top, 1e-30)) * 256.0)
    code = jnp.round(value * (jnp.exp2(level * (-1.0 / 256.0)) * SUM_TOP))
    code = jnp.clip(code, -32767.0, 32767.0)
    out_ref[span, :width] = code.astype(I32).astype(I16)
    out_ref[span, width:] = jnp.broadcast_to(level, (value.shape[0], LANES)).astype(I32).astype(I16)


def unpack(code):
    width = code.shape[-1] - LANES
    level = code[:, width : width + 1].astype(I32).astype(F32)
    factor = jnp.exp2(level * (1.0 / 256.0)) * (1.0 / SUM_TOP)
    return code[:, :width].astype(I32).astype(F32) * factor


def collect_kernel(part, *refs):
    first, middle, last = refs[:4], refs[4:8], refs[8:12]
    sends, own_ref, held = refs[12:15], refs[15], refs[16]
    size = own_ref.shape[0]

    def joined(blocks, span):
        total = blocks[0][span, :]
        for got in blocks[1:]:
            total = total + unpack(got[span, :])
        return total

    held[0] = joined(first, slice(part * size, (part + 1) * size))
    held[1] = joined(middle, slice(0, size))
    held[2] = joined(middle, slice(size, 2 * size))
    held[3] = joined(last, slice(0, size))
    for d in range(4):
        value = held[slot_of(d)]
        if d == 0:
            own_ref[...] = value
        else:
            pack(value, sends[d - 1])


def collect(part, first, middle, last):
    size, width = last[0].shape
    message = jax.ShapeDtypeStruct((size, width + LANES), I16)
    return pl.pallas_call(
        functools.partial(collect_kernel, part),
        out_shape=[message] * 3 + [jax.ShapeDtypeStruct((size, width), F32)],
        in_specs=[vmem()] * 12,
        out_specs=[vmem()] * 4,
        scratch_shapes=[pltpu.VMEM((4, size, width), F32)],
        compiler_params=params(12),
    )(*first, *middle, *last)


def finish_kernel(w_ref, *refs):
    out_ref = refs[-1]
    for part in range(2):
        own, a, b, c = refs[4 * part : 4 * part + 4]
        size = own.shape[0]
        total = own[...] + unpack(a[...]) + unpack(b[...]) + unpack(c[...])
        out_ref[part * size : (part + 1) * size, :] = (total * w_ref[...]).astype(BF16)


def finish(w_scale, parts):
    size, width = parts[0].shape
    return pl.pallas_call(
        finish_kernel,
        out_shape=jax.ShapeDtypeStruct((2 * size, width), BF16),
        in_specs=[vmem()] * 9,
        out_specs=vmem(),
        compiler_params=params(),
        name="finish",
    )(w_scale, *parts)


def along_x(block, apart):
    return lax.ppermute(block, "seq", [(i, (i + 2 * apart) % 8) for i in range(8)])


def other_core(block):
    return lax.ppermute(block, "seq", [(i, i ^ 1) for i in range(8)])


def along_z(blocks):
    got = []
    for apart, block in enumerate(blocks, 1):
        got.append(lax.ppermute(block, "tensor", [(i, (i + 4 * apart) % 16) for i in range(16)]))
    return got


def along_y(blocks):
    got = []
    for apart, block in enumerate(blocks, 1):
        route = [(i, i // 4 * 4 + (i + apart) % 4) for i in range(16)]
        got.append(lax.ppermute(block, "tensor", route))
    return got


def step(hidden, down_int, w_scale, had_small):
    tokens, columns = hidden.shape
    ranks = lax.axis_size("tensor")
    small = had_small.astype(BF16)
    small, hidden = lax.optimization_barrier((small, hidden))
    sent = hidden.reshape(ranks, tokens // ranks, columns)
    whole = lax.all_to_all(sent, "tensor", split_axis=0, concat_axis=0, tiled=True)
    code, weight = rotate(whole.reshape(tokens, columns), small, down_int)
    code = code.reshape(ranks, tokens // ranks, columns + LANES)
    back = lax.all_to_all(code, "tensor", split_axis=0, concat_axis=0, tiled=True)
    own = back.reshape(tokens, columns + LANES)
    act_scale = scale_of(own[:, columns : columns + LANES])[:, 0]

    own_c = other_core(own)
    halves = own.reshape(2, 2, ROWS // 2, columns + LANES)
    own_0 = halves[:, 0].reshape(ROWS, columns + LANES)
    own_1 = halves[:, 1].reshape(ROWS, columns + LANES)
    below_0, above_0 = along_x(own_0, 1), along_x(own_0, -1)
    below_1, above_1 = along_x(own_1, 1), along_x(own_1, -1)
    natural, grouped = (ROWS // 2, ROWS), (2 * ROWS, ROWS // 2)
    codes = [(own, 0), (own, 1), (own_c, 0), (own_c, 1)]
    *sends, kept_0 = product(codes, weight, natural)
    sends, below_0, above_0 = lax.optimization_barrier((sends, below_0, above_0))
    got_0 = along_y(sends)
    far_0 = along_x(below_0, 1)
    codes = [above_0, other_core(above_0), below_0, other_core(below_0)]
    *sends, kept_1 = product([(code, 0) for code in codes], weight, grouped)
    sends, below_1, above_1 = lax.optimization_barrier((sends, below_1, above_1))
    got_1 = along_y(sends)
    far_1 = along_x(above_1, -1)
    codes = [above_1, other_core(above_1), below_1, other_core(below_1)]
    *sends, kept_2 = product([(code, 0) for code in codes], weight, grouped)
    sends, far_0, far_1 = lax.optimization_barrier((sends, far_0, far_1))
    got_2 = along_y(sends)
    codes = [far_0, other_core(far_0), far_1, other_core(far_1)]
    outs = product([(code, 0) for code in codes], weight, grouped, 2)
    got_a, got_b = along_y(outs[:3]), along_y(outs[4:7])
    *sends, own_a = collect(0, [kept_0, *got_0], [kept_1, *got_1], [outs[3], *got_a])
    end_a = along_z(sends)
    *sends, own_b = collect(1, [kept_0, *got_0], [kept_2, *got_2], [outs[7], *got_b])
    end_b = along_z(sends)
    mixed = finish(w_scale[None, :], [own_a, *end_a, own_b, *end_b])
    return (mixed, act_scale)


def solution(mesh):
    return jax.shard_map(
        step,
        mesh=mesh,
        in_specs=(P("seq", "tensor"), P("tensor", "seq"), P("seq"), P()),
        out_specs=(P("tensor", "seq"), P("seq")),
        check_vma=False,
    )
```

```python
import functools
import math

import jax
import jax.numpy as jnp
from jax import lax
from jax.experimental import pallas as pl
from jax.experimental.pallas import tpu as pltpu
from jax.sharding import PartitionSpec as P

FF = 53248
HAD = 52

clip_ratio = 0.9
epsilon = 1e-05

F32, BF16, I16, I32 = jnp.float32, jnp.bfloat16, jnp.int16, jnp.int32
LANES = 128
CODE_TOP = 32767.0
SUM_TOP = 32700.0
BLOCK = 512
ROWS = 64


def vmem():
    return pl.BlockSpec(memory_space=pltpu.VMEM)


def params(mebibytes=12, **more):
    return pltpu.CompilerParams(vmem_limit_bytes=mebibytes * 1024 * 1024, **more)


def slot_of(apart):
    ahead = ((lax.axis_index("tensor") >> 2) + apart - (lax.axis_index("seq") >> 1)) & 3
    return ahead ^ (ahead >> 1)


def place_of(apart):
    return ((lax.axis_index("tensor") + apart) & 3) ^ ((lax.axis_index("seq") & 1) * 2)


def parity_sign(left, right, bits):
    both = left & right
    parity = jnp.zeros(both.shape, I32)
    for shift_bit in range(bits):
        parity = parity ^ (both >> shift_bit & 1)
    return 1 - 2 * parity


def iota(shape, dim):
    return lax.broadcasted_iota(I32, shape, dim)


def block_of(index):
    return jnp.floor((index.astype(F32) + 0.5) * (1.0 / HAD)).astype(I32)


def rotate_kernel(x_ref, had_ref, w_ref, code_ref, held_ref, matrix, stacked, mixed, sem):
    fetch = pltpu.make_async_copy(w_ref, held_ref, sem)
    fetch.start()
    width = matrix.shape[0]
    group = 4 * HAD
    row = iota((group, HAD), 0)
    pick_row = (row - HAD * block_of(row) == iota((group, HAD), 1)).astype(BF16)
    lane = iota((HAD, width), 1)
    pick_lane = (lane - HAD * block_of(lane) == iota((HAD, width), 0)).astype(BF16)
    small = had_ref[...]
    tiled = jnp.dot(small, pick_lane, preferred_element_type=F32).astype(BF16)
    base = jnp.dot(pick_row, tiled, preferred_element_type=F32)
    row_block = block_of(iota((group, width), 0))
    lane_block = block_of(iota((group, width), 1))
    base = base * parity_sign(row_block, lane_block & 3, 2).astype(F32)
    line_block = block_of(iota((8, width), 1)) >> 2
    lines = parity_sign(iota((8, width), 0), line_block, 3).astype(F32)
    for g in range(width // group):
        matrix[g * group : (g + 1) * group, :] = (base * lines[g : g + 1, :]).astype(BF16)
    rows = x_ref.shape[0]
    count = rows // 8
    for half in range(2):
        stacked[half * rows : (half + 1) * rows, :] = x_ref[:, half * width : (half + 1) * width]
    mixed[...] = jnp.dot(stacked[...], matrix[...], preferred_element_type=F32)
    norm_factor = jnp.float32(1.0 / math.sqrt(FF))
    top = jnp.zeros((8, LANES), F32)
    for tile in range(width // LANES):
        span = slice(tile * LANES, (tile + 1) * LANES)
        values = [mixed[8 * t : 8 * t + 8, span] for t in range(2 * count)]
        step = 1
        while step < len(values):
            for low in range(len(values)):
                if not low & step:
                    a, b = values[low], values[low | step]
                    values[low], values[low | step] = a + b, a - b
            step *= 2
        for index, value in enumerate(values):
            value = value * norm_factor
            top = jnp.maximum(top, jnp.abs(value))
            mixed[8 * index : 8 * index + 8, span] = value
    peak = jnp.max(top, axis=1, keepdims=True)
    act_scale = clip_ratio / 7.0 * (peak + epsilon)
    inverse = jnp.broadcast_to(1.0 / act_scale, (8, LANES))
    for t in range(count // 2):
        for tile in range(2 * width // LANES):
            span = slice(tile * LANES, (tile + 1) * LANES)
            half, place = divmod(tile, width // LANES)
            halves = []
            for part in range(2):
                start = half * rows + 16 * t + 8 * part
                value = mixed[start : start + 8, place * LANES : (place + 1) * LANES]
                quant = jnp.clip(value * inverse, -8.0, 7.0)
                root = jnp.sqrt(jnp.abs(quant)) * (CODE_TOP / math.sqrt(8.0))
                halves.append(jnp.round(jnp.where(quant < 0, -root, root)))
            code_ref[16 * t : 16 * t + 16, span] = jnp.concatenate(halves, 0).astype(I32).astype(I16)
    rest = jnp.broadcast_to(act_scale, (8, LANES)) * 4.0
    lane = iota((8, LANES), 1)
    pieces = jnp.zeros((8, LANES), F32)
    for index in range(4):
        whole = jnp.floor(rest)
        pieces = jnp.where(lane == index, whole, pieces)
        rest = (rest - whole) * 16384.0
    extra = jnp.concatenate([pieces, pieces], 0).astype(I32).astype(I16)
    for t in range(count // 2):
        code_ref[16 * t : 16 * t + 16, 2 * width :] = extra
    fetch.wait()


def scale_of(pieces):
    parts = pieces.astype(I32).astype(F32)
    total = parts[:, 3:4] * 2.0**-42 + parts[:, 2:3] * 2.0**-28
    return (total + parts[:, 1:2] * 2.0**-14 + parts[:, 0:1]) * 0.25


def rotate(x, had_small, weight):
    rows, columns = x.shape
    return pl.pallas_call(
        rotate_kernel,
        out_shape=[
            jax.ShapeDtypeStruct((rows, columns + LANES), I16),
            jax.ShapeDtypeStruct(weight.shape, weight.dtype),
        ],
        in_specs=[vmem(), vmem(), pl.BlockSpec(memory_space=pltpu.HBM)],
        out_specs=[vmem(), vmem()],
        scratch_shapes=[
            pltpu.VMEM((columns // 2, columns // 2), BF16),
            pltpu.VMEM((2 * rows, columns // 2), BF16),
            pltpu.VMEM((2 * rows, columns // 2), F32),
            pltpu.SemaphoreType.DMA,
        ],
        compiler_params=params(34),
        name="rotate",
    )(x, had_small, weight)


def product_kernel(strides, groups, *refs):
    count = 2 * groups
    codes, w_ref = refs[:count], refs[count]
    sends, kept, (lhs, total, scale) = refs[count + 1 : count + 4], refs[count + 4], refs[-3:]
    rows = scale.shape[0] // count
    size = kept.shape[0] // groups
    depth, width = w_ref.shape
    for index, ref in enumerate(codes):
        base = index * rows
        scale[base : base + rows, :] = jnp.broadcast_to(scale_of(ref[:, depth:]), (rows, LANES))
        for tile in range(depth // LANES):
            span = slice(tile * LANES, (tile + 1) * LANES)
            level = ref[:, span].astype(I32).astype(F32)
            quant = level * jnp.abs(level) * (8.0 / CODE_TOP**2)
            high = quant.astype(BF16)
            low = (quant - high.astype(F32)).astype(BF16)
            lhs[base : base + rows, span] = high
            lhs[count * rows + base : count * rows + base + rows, span] = low

    def columns(step, carry):
        start = pl.multiple_of(step * BLOCK, BLOCK)
        both = jnp.dot(lhs[...], w_ref[:, pl.ds(start, BLOCK)], preferred_element_type=F32)
        total[:, pl.ds(start, BLOCK)] = (both[: count * rows] + both[count * rows :]) * scale[:, 0:1]
        return carry

    lax.fori_loop(0, width // BLOCK, columns, 0)
    for group in range(groups):
        span = slice(group * size, (group + 1) * size)
        for d in range(4):
            first = pl.multiple_of(group * strides[0] + place_of(d) * strides[1], size)
            value = total[pl.ds(first, size), :]
            if d == 0:
                kept[span, :] = value
            else:
                pack(value, sends[d - 1], span)


def product(codes, weight, strides):
    rows, depth, width = ROWS, *weight.shape
    groups = len(codes) // 2
    size = groups * rows // 2
    message = jax.ShapeDtypeStruct((size, width + LANES), I16)
    outs = [message] * 3 + [jax.ShapeDtypeStruct((size, width), F32)]
    specs = [
        pl.BlockSpec((rows, depth + LANES), functools.partial(lambda index, n: (index, 0), index))
        for _, index in codes
    ]
    return pl.pallas_call(
        functools.partial(product_kernel, strides, groups),
        grid=(1,),
        out_shape=outs,
        in_specs=specs + [vmem()],
        out_specs=[pl.BlockSpec(out.shape, lambda n: (0, 0)) for out in outs],
        scratch_shapes=[
            pltpu.VMEM((4 * groups * rows, depth), BF16),
            pltpu.VMEM((2 * groups * rows, width), F32),
            pltpu.VMEM((2 * groups * rows, LANES), F32),
        ],
        compiler_params=params(26),
        cost_estimate=pl.CostEstimate(
            flops=8 * groups * rows * depth * width,
            bytes_accessed=2 * depth * width,
            transcendentals=0,
        ),
    )(*[array for array, _ in codes], weight)


def pack(value, out_ref, span=slice(None)):
    width = value.shape[-1]
    top = jnp.max(jnp.abs(value), axis=-1, keepdims=True)
    level = jnp.ceil(jnp.log2(jnp.maximum(top, 1e-30)) * 256.0)
    code = jnp.round(value * (jnp.exp2(level * (-1.0 / 256.0)) * SUM_TOP))
    code = jnp.clip(code, -32767.0, 32767.0)
    out_ref[span, :width] = code.astype(I32).astype(I16)
    out_ref[span, width:] = jnp.broadcast_to(level, (value.shape[0], LANES)).astype(I32).astype(I16)


def unpack(code):
    width = code.shape[-1] - LANES
    level = code[:, width : width + 1].astype(I32).astype(F32)
    factor = jnp.exp2(level * (1.0 / 256.0)) * (1.0 / SUM_TOP)
    return code[:, :width].astype(I32).astype(F32) * factor


def collect_kernel(part, *refs):
    first, middle, last = refs[:4], refs[4:8], refs[8:12]
    sends, own_ref, held = refs[12:15], refs[15], refs[16]
    size = own_ref.shape[0]

    def joined(blocks, span):
        total = blocks[0][span, :]
        for got in blocks[1:]:
            total = total + unpack(got[span, :])
        return total

    held[0] = joined(first, slice(part * size, (part + 1) * size))
    held[1] = joined(middle, slice(0, size))
    held[2] = joined(middle, slice(size, 2 * size))
    held[3] = joined(last, slice(0, size))
    for d in range(4):
        value = held[slot_of(d)]
        if d == 0:
            own_ref[...] = value
        else:
            pack(value, sends[d - 1])


def collect(part, first, middle, last):
    size, width = last[0].shape
    message = jax.ShapeDtypeStruct((size, width + LANES), I16)
    return pl.pallas_call(
        functools.partial(collect_kernel, part),
        out_shape=[message] * 3 + [jax.ShapeDtypeStruct((size, width), F32)],
        in_specs=[vmem()] * 12,
        out_specs=[vmem()] * 4,
        scratch_shapes=[pltpu.VMEM((4, size, width), F32)],
        compiler_params=params(12),
    )(*first, *middle, *last)


def finish_kernel(w_ref, *refs):
    out_ref = refs[-1]
    for part in range(2):
        own, a, b, c = refs[4 * part : 4 * part + 4]
        size = own.shape[0]
        total = own[...] + unpack(a[...]) + unpack(b[...]) + unpack(c[...])
        out_ref[part * size : (part + 1) * size, :] = (total * w_ref[...]).astype(BF16)


def finish(w_scale, parts):
    size, width = parts[0].shape
    return pl.pallas_call(
        finish_kernel,
        out_shape=jax.ShapeDtypeStruct((2 * size, width), BF16),
        in_specs=[vmem()] * 9,
        out_specs=vmem(),
        compiler_params=params(),
        name="finish",
    )(w_scale, *parts)


def along_x(block, apart):
    return lax.ppermute(block, "seq", [(i, (i + 2 * apart) % 8) for i in range(8)])


def other_core(block):
    return lax.ppermute(block, "seq", [(i, i ^ 1) for i in range(8)])


def along_z(blocks):
    got = []
    for apart, block in enumerate(blocks, 1):
        got.append(lax.ppermute(block, "tensor", [(i, (i + 4 * apart) % 16) for i in range(16)]))
    return got


def along_y(blocks):
    got = []
    for apart, block in enumerate(blocks, 1):
        route = [(i, i // 4 * 4 + (i + apart) % 4) for i in range(16)]
        got.append(lax.ppermute(block, "tensor", route))
    return got


def step(hidden, down_int, w_scale, had_small):
    tokens, columns = hidden.shape
    ranks = lax.axis_size("tensor")
    small = had_small.astype(BF16)
    small, hidden = lax.optimization_barrier((small, hidden))
    sent = hidden.reshape(ranks, tokens // ranks, columns)
    whole = lax.all_to_all(sent, "tensor", split_axis=0, concat_axis=0, tiled=True)
    code, weight = rotate(whole.reshape(tokens, columns), small, down_int)
    code = code.reshape(ranks, tokens // ranks, columns + LANES)
    back = lax.all_to_all(code, "tensor", split_axis=0, concat_axis=0, tiled=True)
    own = back.reshape(tokens, columns + LANES)
    act_scale = scale_of(own[:, columns : columns + LANES])[:, 0]

    own_c = other_core(own)
    halves = own.reshape(2, 2, ROWS // 2, columns + LANES)
    own_0 = halves[:, 0].reshape(ROWS, columns + LANES)
    own_1 = halves[:, 1].reshape(ROWS, columns + LANES)
    below_0, above_0 = along_x(own_0, 1), along_x(own_0, -1)
    below_1, above_1 = along_x(own_1, 1), along_x(own_1, -1)
    natural, grouped = (ROWS // 2, ROWS), (2 * ROWS, ROWS // 2)
    codes = [(own, 0), (own, 1), (own_c, 0), (own_c, 1)]
    *sends, kept_0 = product(codes, weight, natural)
    sends, below_0, above_0 = lax.optimization_barrier((sends, below_0, above_0))
    got_0 = along_y(sends)
    far_0, far_1 = along_x(own_0, 2), along_x(own_1, 2)
    codes = [above_0, other_core(above_0), below_0, other_core(below_0)]
    *sends, kept_1 = product([(code, 0) for code in codes], weight, grouped)
    sends, below_1, above_1 = lax.optimization_barrier((sends, below_1, above_1))
    got_1 = along_y(sends)
    codes = [above_1, other_core(above_1), below_1, other_core(below_1)]
    *sends, kept_2 = product([(code, 0) for code in codes], weight, grouped)
    sends, far_0 = lax.optimization_barrier((sends, far_0))
    got_2 = along_y(sends)
    *sends, kept_a = product([(far_0, 0), (other_core(far_0), 0)], weight, grouped)
    sends, far_1 = lax.optimization_barrier((sends, far_1))
    got_a = along_y(sends)
    *sends, kept_b = product([(far_1, 0), (other_core(far_1), 0)], weight, grouped)
    got_b = along_y(sends)
    *sends, own_a = collect(0, [kept_0, *got_0], [kept_1, *got_1], [kept_a, *got_a])
    end_a = along_z(sends)
    *sends, own_b = collect(1, [kept_0, *got_0], [kept_2, *got_2], [kept_b, *got_b])
    end_b = along_z(sends)
    mixed = finish(w_scale[None, :], [own_a, *end_a, own_b, *end_b])
    return (mixed, act_scale)


def solution(mesh):
    return jax.shard_map(
        step,
        mesh=mesh,
        in_specs=(P("seq", "tensor"), P("tensor", "seq"), P("seq"), P()),
        out_specs=(P("tensor", "seq"), P("seq")),
        check_vma=False,
    )
```

```python
import functools
import math

import jax
import jax.numpy as jnp
from jax import lax
from jax.experimental import pallas as pl
from jax.experimental.pallas import tpu as pltpu
from jax.sharding import PartitionSpec as P

FF = 53248
HAD = 52

clip_ratio = 0.9
epsilon = 1e-05

F32, BF16, I16, I32 = jnp.float32, jnp.bfloat16, jnp.int16, jnp.int32
LANES = 128
CODE_TOP = 32767.0
SUM_TOP = 32700.0
BLOCK = 512
FETCH_ROOM = 28
ROWS = 64


def vmem():
    return pl.BlockSpec(memory_space=pltpu.VMEM)


def params(mebibytes=12, **more):
    return pltpu.CompilerParams(vmem_limit_bytes=mebibytes * 1024 * 1024, **more)


def slot_of(apart):
    ahead = ((lax.axis_index("tensor") >> 2) + apart - (lax.axis_index("seq") >> 1)) & 3
    return ahead ^ (ahead >> 1)


def place_of(apart):
    return ((lax.axis_index("tensor") + apart) & 3) ^ ((lax.axis_index("seq") & 1) * 2)


def parity_sign(left, right, bits):
    both = left & right
    parity = jnp.zeros(both.shape, I32)
    for shift_bit in range(bits):
        parity = parity ^ (both >> shift_bit & 1)
    return 1 - 2 * parity


def iota(shape, dim):
    return lax.broadcasted_iota(I32, shape, dim)


def block_of(index):
    return jnp.floor((index.astype(F32) + 0.5) * (1.0 / HAD)).astype(I32)


def rotate_kernel(x_ref, had_ref, code_ref, matrix, stacked, mixed):
    width = matrix.shape[0]
    group = 4 * HAD
    row = iota((group, HAD), 0)
    pick_row = (row - HAD * block_of(row) == iota((group, HAD), 1)).astype(BF16)
    lane = iota((HAD, width), 1)
    pick_lane = (lane - HAD * block_of(lane) == iota((HAD, width), 0)).astype(BF16)
    small = had_ref[...]
    tiled = jnp.dot(small, pick_lane, preferred_element_type=F32).astype(BF16)
    base = jnp.dot(pick_row, tiled, preferred_element_type=F32)
    row_block = block_of(iota((group, width), 0))
    lane_block = block_of(iota((group, width), 1))
    base = base * parity_sign(row_block, lane_block & 3, 2).astype(F32)
    line_block = block_of(iota((8, width), 1)) >> 2
    lines = parity_sign(iota((8, width), 0), line_block, 3).astype(F32)
    for g in range(width // group):
        matrix[g * group : (g + 1) * group, :] = (base * lines[g : g + 1, :]).astype(BF16)
    rows = x_ref.shape[0]
    count = rows // 8
    for half in range(2):
        stacked[half * rows : (half + 1) * rows, :] = x_ref[:, half * width : (half + 1) * width]
    mixed[...] = jnp.dot(stacked[...], matrix[...], preferred_element_type=F32)
    norm_factor = jnp.float32(1.0 / math.sqrt(FF))
    top = jnp.zeros((8, LANES), F32)
    for tile in range(width // LANES):
        span = slice(tile * LANES, (tile + 1) * LANES)
        values = [mixed[8 * t : 8 * t + 8, span] for t in range(2 * count)]
        step = 1
        while step < len(values):
            for low in range(len(values)):
                if not low & step:
                    a, b = values[low], values[low | step]
                    values[low], values[low | step] = a + b, a - b
            step *= 2
        for index, value in enumerate(values):
            value = value * norm_factor
            top = jnp.maximum(top, jnp.abs(value))
            mixed[8 * index : 8 * index + 8, span] = value
    peak = jnp.max(top, axis=1, keepdims=True)
    act_scale = clip_ratio / 7.0 * (peak + epsilon)
    inverse = jnp.broadcast_to(1.0 / act_scale, (8, LANES))
    for t in range(count // 2):
        for tile in range(2 * width // LANES):
            span = slice(tile * LANES, (tile + 1) * LANES)
            half, place = divmod(tile, width // LANES)
            halves = []
            for part in range(2):
                start = half * rows + 16 * t + 8 * part
                value = mixed[start : start + 8, place * LANES : (place + 1) * LANES]
                quant = jnp.clip(value * inverse, -8.0, 7.0)
                root = jnp.sqrt(jnp.abs(quant)) * (CODE_TOP / math.sqrt(8.0))
                halves.append(jnp.round(jnp.where(quant < 0, -root, root)))
            code_ref[16 * t : 16 * t + 16, span] = jnp.concatenate(halves, 0).astype(I32).astype(I16)
    rest = jnp.broadcast_to(act_scale, (8, LANES)) * 4.0
    lane = iota((8, LANES), 1)
    pieces = jnp.zeros((8, LANES), F32)
    for index in range(4):
        whole = jnp.floor(rest)
        pieces = jnp.where(lane == index, whole, pieces)
        rest = (rest - whole) * 16384.0
    extra = jnp.concatenate([pieces, pieces], 0).astype(I32).astype(I16)
    for t in range(count // 2):
        code_ref[16 * t : 16 * t + 16, 2 * width :] = extra


def scale_of(pieces):
    parts = pieces.astype(I32).astype(F32)
    total = parts[:, 3:4] * 2.0**-42 + parts[:, 2:3] * 2.0**-28
    return (total + parts[:, 1:2] * 2.0**-14 + parts[:, 0:1]) * 0.25


def rotate(x, had_small):
    rows, columns = x.shape
    return pl.pallas_call(
        rotate_kernel,
        out_shape=jax.ShapeDtypeStruct((rows, columns + LANES), I16),
        in_specs=[vmem(), vmem()],
        out_specs=vmem(),
        scratch_shapes=[
            pltpu.VMEM((columns // 2, columns // 2), BF16),
            pltpu.VMEM((2 * rows, columns // 2), BF16),
            pltpu.VMEM((2 * rows, columns // 2), F32),
        ],
        compiler_params=params(24),
        name="rotate",
    )(x, had_small)


def product_kernel(strides, groups, fetched, parts, *refs):
    count = 2 * groups
    codes, w_ref = refs[:count], refs[count]
    last = count + 1 + 4 * parts
    outs = refs[count + 1 : last]
    lhs, total, scale = refs[last + fetched : last + 3 + fetched]
    rows = scale.shape[0] // count
    size = rows // 2
    depth, width = w_ref.shape
    fetches = []
    if fetched:
        far_ref, w_ref, sem = w_ref, refs[last], refs[-1]
        for step in range(width // BLOCK):
            span = slice(step * BLOCK, (step + 1) * BLOCK)
            fetches.append(pltpu.make_async_copy(far_ref.at[:, span], w_ref.at[:, span], sem.at[step]))
            fetches[-1].start()
    for index, ref in enumerate(codes):
        base = index * rows
        scale[base : base + rows, :] = jnp.broadcast_to(scale_of(ref[:, depth:]), (rows, LANES))
        for tile in range(depth // LANES):
            span = slice(tile * LANES, (tile + 1) * LANES)
            level = ref[:, span].astype(I32).astype(F32)
            quant = level * jnp.abs(level) * (8.0 / CODE_TOP**2)
            high = quant.astype(BF16)
            low = (quant - high.astype(F32)).astype(BF16)
            lhs[base : base + rows, span] = high
            lhs[count * rows + base : count * rows + base + rows, span] = low

    def columns(step, carry):
        if fetched:
            start = step * BLOCK
            fetches[step].wait()
        else:
            start = pl.multiple_of(step * BLOCK, BLOCK)
        both = jnp.dot(lhs[...], w_ref[:, pl.ds(start, BLOCK)], preferred_element_type=F32)
        total[:, pl.ds(start, BLOCK)] = (both[: count * rows] + both[count * rows :]) * scale[:, 0:1]
        return carry

    if fetched:
        for step in range(width // BLOCK):
            columns(step, 0)
    else:
        lax.fori_loop(0, width // BLOCK, columns, 0)
    for group in range(groups):
        span = slice(group * size, (group + 1) * size) if parts == 1 else slice(None)
        chosen = outs if parts == 1 else outs[4 * group : 4 * group + 4]
        for d in range(4):
            first = pl.multiple_of(group * strides[0] + place_of(d) * strides[1], size)
            value = total[pl.ds(first, size), :]
            if d == 0:
                chosen[3][span, :] = value
            else:
                pack(value, chosen[d - 1], span)


def product(codes, weight, strides, fetched=False, parts=1):
    rows, depth, width = ROWS, *weight.shape
    groups = len(codes) // 2
    size = groups * rows // 2 // parts
    message = jax.ShapeDtypeStruct((size, width + LANES), I16)
    outs = ([message] * 3 + [jax.ShapeDtypeStruct((size, width), F32)]) * parts
    specs = [
        pl.BlockSpec((rows, depth + LANES), functools.partial(lambda index, n: (index, 0), index))
        for _, index in codes
    ]
    out_specs = [pl.BlockSpec(out.shape, lambda n: (0, 0)) for out in outs]
    if fetched:
        outs = outs + [jax.ShapeDtypeStruct(weight.shape, weight.dtype)]
        out_specs = out_specs + [vmem()]
    return pl.pallas_call(
        functools.partial(product_kernel, strides, groups, int(fetched), parts),
        grid=(1,),
        out_shape=outs,
        in_specs=specs + [pl.BlockSpec(memory_space=pltpu.HBM) if fetched else vmem()],
        out_specs=out_specs,
        scratch_shapes=[
            pltpu.VMEM((4 * groups * rows, depth), BF16),
            pltpu.VMEM((2 * groups * rows, width), F32),
            pltpu.VMEM((2 * groups * rows, LANES), F32),
        ]
        + [pltpu.SemaphoreType.DMA((width // BLOCK,))] * fetched,
        compiler_params=params(FETCH_ROOM if fetched else 26),
        cost_estimate=pl.CostEstimate(
            flops=8 * groups * rows * depth * width,
            bytes_accessed=2 * depth * width,
            transcendentals=0,
        ),
    )(*[array for array, _ in codes], weight)


def pack(value, out_ref, span=slice(None)):
    width = value.shape[-1]
    top = jnp.max(jnp.abs(value), axis=-1, keepdims=True)
    level = jnp.ceil(jnp.log2(jnp.maximum(top, 1e-30)) * 256.0)
    code = jnp.round(value * (jnp.exp2(level * (-1.0 / 256.0)) * SUM_TOP))
    code = jnp.clip(code, -32767.0, 32767.0)
    out_ref[span, :width] = code.astype(I32).astype(I16)
    out_ref[span, width:] = jnp.broadcast_to(level, (value.shape[0], LANES)).astype(I32).astype(I16)


def unpack(code):
    width = code.shape[-1] - LANES
    level = code[:, width : width + 1].astype(I32).astype(F32)
    factor = jnp.exp2(level * (1.0 / 256.0)) * (1.0 / SUM_TOP)
    return code[:, :width].astype(I32).astype(F32) * factor


def collect_kernel(part, *refs):
    first, middle, last = refs[:4], refs[4:8], refs[8:12]
    sends, own_ref, held = refs[12:15], refs[15], refs[16]
    size = own_ref.shape[0]

    def joined(blocks, span):
        total = blocks[0][span, :]
        for got in blocks[1:]:
            total = total + unpack(got[span, :])
        return total

    held[0] = joined(first, slice(part * size, (part + 1) * size))
    held[1] = joined(middle, slice(0, size))
    held[2] = joined(middle, slice(size, 2 * size))
    held[3] = joined(last, slice(0, size))
    for d in range(4):
        value = held[slot_of(d)]
        if d == 0:
            own_ref[...] = value
        else:
            pack(value, sends[d - 1])


def collect(part, first, middle, last):
    size, width = last[0].shape
    message = jax.ShapeDtypeStruct((size, width + LANES), I16)
    return pl.pallas_call(
        functools.partial(collect_kernel, part),
        out_shape=[message] * 3 + [jax.ShapeDtypeStruct((size, width), F32)],
        in_specs=[vmem()] * 12,
        out_specs=[vmem()] * 4,
        scratch_shapes=[pltpu.VMEM((4, size, width), F32)],
        compiler_params=params(12),
    )(*first, *middle, *last)


def finish_kernel(w_ref, *refs):
    out_ref = refs[-1]
    for part in range(2):
        own, a, b, c = refs[4 * part : 4 * part + 4]
        size = own.shape[0]
        total = own[...] + unpack(a[...]) + unpack(b[...]) + unpack(c[...])
        out_ref[part * size : (part + 1) * size, :] = (total * w_ref[...]).astype(BF16)


def finish(w_scale, parts):
    size, width = parts[0].shape
    return pl.pallas_call(
        finish_kernel,
        out_shape=jax.ShapeDtypeStruct((2 * size, width), BF16),
        in_specs=[vmem()] * 9,
        out_specs=vmem(),
        compiler_params=params(),
        name="finish",
    )(w_scale, *parts)


def along_x(block, apart):
    return lax.ppermute(block, "seq", [(i, (i + 2 * apart) % 8) for i in range(8)])


def other_core(block):
    return lax.ppermute(block, "seq", [(i, i ^ 1) for i in range(8)])


def along_z(blocks):
    got = []
    for apart, block in enumerate(blocks, 1):
        got.append(lax.ppermute(block, "tensor", [(i, (i + 4 * apart) % 16) for i in range(16)]))
    return got


def along_y(blocks):
    got = []
    for apart, block in enumerate(blocks, 1):
        route = [(i, i // 4 * 4 + (i + apart) % 4) for i in range(16)]
        got.append(lax.ppermute(block, "tensor", route))
    return got


def step(hidden, down_int, w_scale, had_small):
    tokens, columns = hidden.shape
    ranks = lax.axis_size("tensor")
    small = had_small.astype(BF16)
    small, hidden = lax.optimization_barrier((small, hidden))
    sent = hidden.reshape(ranks, tokens // ranks, columns)
    whole = lax.all_to_all(sent, "tensor", split_axis=0, concat_axis=0, tiled=True)
    code = rotate(whole.reshape(tokens, columns), small)
    code = code.reshape(ranks, tokens // ranks, columns + LANES)
    back = lax.all_to_all(code, "tensor", split_axis=0, concat_axis=0, tiled=True)
    own = back.reshape(tokens, columns + LANES)
    act_scale = scale_of(own[:, columns : columns + LANES])[:, 0]

    own_c = other_core(own)
    halves = own.reshape(2, 2, ROWS // 2, columns + LANES)
    own_0 = halves[:, 0].reshape(ROWS, columns + LANES)
    own_1 = halves[:, 1].reshape(ROWS, columns + LANES)
    below_0, above_0 = along_x(own_0, 1), along_x(own_0, -1)
    below_1, above_1 = along_x(own_1, 1), along_x(own_1, -1)
    natural, grouped = (ROWS // 2, ROWS), (2 * ROWS, ROWS // 2)
    codes = [(own, 0), (own, 1), (own_c, 0), (own_c, 1)]
    *sends, kept_0, weight = product(codes, down_int, natural, True)
    sends, below_0, above_0 = lax.optimization_barrier((sends, below_0, above_0))
    got_0 = along_y(sends)
    codes = [above_0, other_core(above_0), below_0, other_core(below_0)]
    *sends, kept_1 = product([(code, 0) for code in codes], weight, grouped)
    sends, below_0, below_1, above_1 = lax.optimization_barrier((sends, below_0, below_1, above_1))
    got_1 = along_y(sends)
    far_0, far_1 = along_x(below_0, 1), along_x(above_1, -1)
    codes = [above_1, other_core(above_1), below_1, other_core(below_1)]
    *sends, kept_2 = product([(code, 0) for code in codes], weight, grouped)
    sends, far_0, far_1 = lax.optimization_barrier((sends, far_0, far_1))
    got_2 = along_y(sends)
    codes = [far_0, other_core(far_0), far_1, other_core(far_1)]
    outs = product([(code, 0) for code in codes], weight, grouped, parts=2)
    got_a, got_b = along_y(outs[:3]), along_y(outs[4:7])
    kept_a, kept_b = outs[3], outs[7]
    *sends, own_a = collect(0, [kept_0, *got_0], [kept_1, *got_1], [kept_a, *got_a])
    end_a = along_z(sends)
    *sends, own_b = collect(1, [kept_0, *got_0], [kept_2, *got_2], [kept_b, *got_b])
    end_b = along_z(sends)
    mixed = finish(w_scale[None, :], [own_a, *end_a, own_b, *end_b])
    return (mixed, act_scale)


def solution(mesh):
    return jax.shard_map(
        step,
        mesh=mesh,
        in_specs=(P("seq", "tensor"), P("tensor", "seq"), P("seq"), P()),
        out_specs=(P("tensor", "seq"), P("seq")),
        check_vma=False,
    )
```

```python
import functools
import math

import jax
import jax.numpy as jnp
from jax import lax
from jax.experimental import pallas as pl
from jax.experimental.pallas import tpu as pltpu
from jax.sharding import PartitionSpec as P

FF = 53248
HAD = 52

clip_ratio = 0.9
epsilon = 1e-05

F32, BF16, I16, I32 = jnp.float32, jnp.bfloat16, jnp.int16, jnp.int32
LANES = 128
CODE_TOP = 32767.0
SUM_TOP = 32700.0
BLOCK = 512
FIRST = 512
CUTS = (1024, 1792, 2560)
ROWS = 64


def vmem():
    return pl.BlockSpec(memory_space=pltpu.VMEM)


def params(mebibytes=12, **more):
    return pltpu.CompilerParams(vmem_limit_bytes=mebibytes * 1024 * 1024, **more)


def slot_of(apart):
    ahead = ((lax.axis_index("tensor") >> 2) + apart - (lax.axis_index("seq") >> 1)) & 3
    return ahead ^ (ahead >> 1)


def place_of(apart):
    return ((lax.axis_index("tensor") + apart) & 3) ^ ((lax.axis_index("seq") & 1) * 2)


def parity_sign(left, right, bits):
    both = left & right
    parity = jnp.zeros(both.shape, I32)
    for shift_bit in range(bits):
        parity = parity ^ (both >> shift_bit & 1)
    return 1 - 2 * parity


def iota(shape, dim):
    return lax.broadcasted_iota(I32, shape, dim)


def block_of(index):
    return jnp.floor((index.astype(F32) + 0.5) * (1.0 / HAD)).astype(I32)


def rotate_kernel(x_ref, had_ref, w_ref, code_ref, held_ref, matrix, mixed, sem):
    fetch = pltpu.make_async_copy(w_ref, held_ref, sem)
    fetch.start()
    width = matrix.shape[0]
    group = 4 * HAD
    row = iota((group, HAD), 0)
    pick_row = (row - HAD * block_of(row) == iota((group, HAD), 1)).astype(BF16)
    lane = iota((HAD, width), 1)
    pick_lane = (lane - HAD * block_of(lane) == iota((HAD, width), 0)).astype(BF16)
    small = had_ref[...]
    tiled = jnp.dot(small, pick_lane, preferred_element_type=F32).astype(BF16)
    base = jnp.dot(pick_row, tiled, preferred_element_type=F32)
    row_block = block_of(iota((group, width), 0))
    lane_block = block_of(iota((group, width), 1))
    base = base * parity_sign(row_block, lane_block & 3, 2).astype(F32)
    line_block = block_of(iota((8, width), 1)) >> 2
    lines = parity_sign(iota((8, width), 0), line_block, 3).astype(F32)
    for g in range(width // group):
        matrix[g * group : (g + 1) * group, :] = (base * lines[g : g + 1, :]).astype(BF16)
    rows = x_ref.shape[0]
    count = rows // 8
    for half in range(2):
        span = slice(half * width, (half + 1) * width)
        mixed[:, span] = jnp.dot(x_ref[:, span], matrix[...], preferred_element_type=F32)
    norm_factor = jnp.float32(1.0 / math.sqrt(FF))
    top = jnp.zeros((8, LANES), F32)
    for tile in range(width // LANES):
        columns = [slice(half * width + tile * LANES, half * width + (tile + 1) * LANES) for half in range(2)]
        values = [mixed[8 * t : 8 * t + 8, span] for span in columns for t in range(count)]
        step = 1
        while step < len(values):
            for low in range(len(values)):
                if not low & step:
                    a, b = values[low], values[low | step]
                    values[low], values[low | step] = a + b, a - b
            step *= 2
        for index, value in enumerate(values):
            half, t = index // count, index % count
            value = value * norm_factor
            top = jnp.maximum(top, jnp.abs(value))
            mixed[8 * t : 8 * t + 8, columns[half]] = value
    peak = jnp.max(top, axis=1, keepdims=True)
    act_scale = clip_ratio / 7.0 * (peak + epsilon)
    inverse = jnp.broadcast_to(1.0 / act_scale, (8, LANES))
    for t in range(count // 2):
        for tile in range(2 * width // LANES):
            span = slice(tile * LANES, (tile + 1) * LANES)
            halves = []
            for part in range(2):
                start = 16 * t + 8 * part
                quant = jnp.clip(mixed[start : start + 8, span] * inverse, -8.0, 7.0)
                root = jnp.sqrt(jnp.abs(quant)) * (CODE_TOP / math.sqrt(8.0))
                halves.append(jnp.round(jnp.where(quant < 0, -root, root)))
            code_ref[16 * t : 16 * t + 16, span] = jnp.concatenate(halves, 0).astype(I32).astype(I16)
    rest = jnp.broadcast_to(act_scale, (8, LANES)) * 4.0
    lane = iota((8, LANES), 1)
    pieces = jnp.zeros((8, LANES), F32)
    for index in range(4):
        whole = jnp.floor(rest)
        pieces = jnp.where(lane == index, whole, pieces)
        rest = (rest - whole) * 16384.0
    extra = jnp.concatenate([pieces, pieces], 0).astype(I32).astype(I16)
    for t in range(count // 2):
        code_ref[16 * t : 16 * t + 16, 2 * width :] = extra
    fetch.wait()


def scale_of(pieces):
    parts = pieces.astype(I32).astype(F32)
    total = parts[:, 3:4] * 2.0**-42 + parts[:, 2:3] * 2.0**-28
    return (total + parts[:, 1:2] * 2.0**-14 + parts[:, 0:1]) * 0.25


def rotate(x, had_small, weight):
    rows, columns = x.shape
    return pl.pallas_call(
        rotate_kernel,
        out_shape=[
            jax.ShapeDtypeStruct((rows, columns + LANES), I16),
            jax.ShapeDtypeStruct(weight.shape, weight.dtype),
        ],
        in_specs=[vmem(), vmem(), pl.BlockSpec(memory_space=pltpu.HBM)],
        out_specs=[vmem(), vmem()],
        scratch_shapes=[
            pltpu.VMEM((columns // 2, columns // 2), BF16),
            pltpu.VMEM((rows, columns), F32),
            pltpu.SemaphoreType.DMA,
        ],
        compiler_params=params(34),
        name="rotate",
    )(x, had_small, weight)


def product_kernel(strides, parts, *refs):
    codes, w_ref = refs[:4], refs[4]
    outs, (lhs, total, scale) = refs[5:-3], refs[-3:]
    rows = scale.shape[0] // 4
    size = rows // 2
    depth, width = w_ref.shape
    for index, ref in enumerate(codes):
        base = index * rows
        scale[base : base + rows, :] = jnp.broadcast_to(scale_of(ref[:, depth:]), (rows, LANES))
    both = None
    edges = (0, *CUTS, depth)
    for low, high in zip(edges[:-1], edges[1:]):
        for index, ref in enumerate(codes):
            base = index * rows
            for start in range(low, high, LANES):
                span = slice(start, start + LANES)
                level = ref[:, span].astype(I32).astype(F32)
                quant = level * jnp.abs(level) * (8.0 / CODE_TOP**2)
                head = quant.astype(BF16)
                lhs[base : base + rows, span] = head
                tail = (quant - head.astype(F32)).astype(BF16)
                lhs[4 * rows + base : 4 * rows + base + rows, span] = tail
        piece = jnp.dot(lhs[:, low:high], w_ref[low:high, :FIRST], preferred_element_type=F32)
        both = piece if both is None else both + piece
    total[:, :FIRST] = (both[: 4 * rows] + both[4 * rows :]) * scale[:, 0:1]

    def columns(step, carry):
        start = pl.multiple_of(FIRST + step * BLOCK, LANES)
        both = jnp.dot(lhs[...], w_ref[:, pl.ds(start, BLOCK)], preferred_element_type=F32)
        total[:, pl.ds(start, BLOCK)] = (both[: 4 * rows] + both[4 * rows :]) * scale[:, 0:1]
        return carry

    lax.fori_loop(0, (width - FIRST) // BLOCK, columns, 0)
    for group in range(2):
        chosen = outs if parts == 1 else outs[4 * group : 4 * group + 4]
        span = slice(group * size, (group + 1) * size) if parts == 1 else slice(None)
        for d in range(4):
            first = pl.multiple_of(group * strides[0] + place_of(d) * strides[1], size)
            value = total[pl.ds(first, size), :]
            if d == 0:
                chosen[3][span, :] = value
            else:
                pack(value, chosen[d - 1], span)


def product(codes, weight, strides, parts=1):
    rows = ROWS
    depth, width = weight.shape
    size = rows // parts
    outs = [jax.ShapeDtypeStruct((size, width + LANES), I16)] * 3 + [jax.ShapeDtypeStruct((size, width), F32)]
    outs = outs * parts
    specs = [
        pl.BlockSpec((rows, depth + LANES), functools.partial(lambda index, n: (index, 0), index))
        for _, index in codes
    ]
    return pl.pallas_call(
        functools.partial(product_kernel, strides, parts),
        grid=(1,),
        out_shape=outs,
        in_specs=specs + [vmem()],
        out_specs=[pl.BlockSpec(out.shape, lambda n: (0, 0)) for out in outs],
        scratch_shapes=[
            pltpu.VMEM((8 * rows, depth), BF16),
            pltpu.VMEM((4 * rows, width), F32),
            pltpu.VMEM((4 * rows, LANES), F32),
        ],
        compiler_params=params(26),
        cost_estimate=pl.CostEstimate(
            flops=16 * rows * depth * width,
            bytes_accessed=2 * depth * width,
            transcendentals=0,
        ),
    )(*[array for array, _ in codes], weight)


def pack(value, out_ref, span=slice(None)):
    width = value.shape[-1]
    top = jnp.max(jnp.abs(value), axis=-1, keepdims=True)
    level = jnp.ceil(jnp.log2(jnp.maximum(top, 1e-30)) * 256.0)
    code = jnp.round(value * (jnp.exp2(level * (-1.0 / 256.0)) * SUM_TOP))
    code = jnp.clip(code, -32767.0, 32767.0)
    out_ref[span, :width] = code.astype(I32).astype(I16)
    out_ref[span, width:] = jnp.broadcast_to(level, (value.shape[0], LANES)).astype(I32).astype(I16)


def unpack(code):
    width = code.shape[-1] - LANES
    level = code[:, width : width + 1].astype(I32).astype(F32)
    factor = jnp.exp2(level * (1.0 / 256.0)) * (1.0 / SUM_TOP)
    return code[:, :width].astype(I32).astype(F32) * factor


def collect_kernel(part, *refs):
    first, middle, last = refs[:4], refs[4:8], refs[8:12]
    sends, own_ref, held = refs[12:15], refs[15], refs[16]
    size = own_ref.shape[0]

    def joined(blocks, span):
        total = blocks[0][span, :]
        for got in blocks[1:]:
            total = total + unpack(got[span, :])
        return total

    held[0] = joined(first, slice(part * size, (part + 1) * size))
    held[1] = joined(middle, slice(0, size))
    held[2] = joined(middle, slice(size, 2 * size))
    held[3] = joined(last, slice(0, size))
    for d in range(4):
        value = held[slot_of(d)]
        if d == 0:
            own_ref[...] = value
        else:
            pack(value, sends[d - 1])


def collect(part, first, middle, last):
    size, width = last[0].shape
    message = jax.ShapeDtypeStruct((size, width + LANES), I16)
    return pl.pallas_call(
        functools.partial(collect_kernel, part),
        out_shape=[message] * 3 + [jax.ShapeDtypeStruct((size, width), F32)],
        in_specs=[vmem()] * 12,
        out_specs=[vmem()] * 4,
        scratch_shapes=[pltpu.VMEM((4, size, width), F32)],
        compiler_params=params(12),
    )(*first, *middle, *last)


def finish_kernel(w_ref, *refs):
    out_ref = refs[-1]
    for part in range(2):
        own, a, b, c = refs[4 * part : 4 * part + 4]
        size = own.shape[0]
        total = own[...] + unpack(a[...]) + unpack(b[...]) + unpack(c[...])
        out_ref[part * size : (part + 1) * size, :] = (total * w_ref[...]).astype(BF16)


def finish(w_scale, parts):
    size, width = parts[0].shape
    return pl.pallas_call(
        finish_kernel,
        out_shape=jax.ShapeDtypeStruct((2 * size, width), BF16),
        in_specs=[vmem()] * 9,
        out_specs=vmem(),
        compiler_params=params(),
        name="finish",
    )(w_scale, *parts)


def along_x(block, apart):
    return lax.ppermute(block, "seq", [(i, (i + 2 * apart) % 8) for i in range(8)])


def other_core(block):
    return lax.ppermute(block, "seq", [(i, i ^ 1) for i in range(8)])


def along_z(blocks):
    got = []
    for apart, block in enumerate(blocks, 1):
        got.append(lax.ppermute(block, "tensor", [(i, (i + 4 * apart) % 16) for i in range(16)]))
    return got


def along_y(blocks):
    got = []
    for apart, block in enumerate(blocks, 1):
        route = [(i, i // 4 * 4 + (i + apart) % 4) for i in range(16)]
        got.append(lax.ppermute(block, "tensor", route))
    return got


def step(hidden, down_int, w_scale, had_small):
    tokens, columns = hidden.shape
    ranks = lax.axis_size("tensor")
    small = had_small.astype(BF16)
    small, hidden = lax.optimization_barrier((small, hidden))
    sent = hidden.reshape(ranks, tokens // ranks, columns)
    whole = lax.all_to_all(sent, "tensor", split_axis=0, concat_axis=0, tiled=True)
    code, weight = rotate(whole.reshape(tokens, columns), small, down_int)
    code = code.reshape(ranks, tokens // ranks, columns + LANES)
    back = lax.all_to_all(code, "tensor", split_axis=0, concat_axis=0, tiled=True)
    own = back.reshape(tokens, columns + LANES)
    act_scale = scale_of(own[:, columns : columns + LANES])[:, 0]

    own_c = other_core(own)
    halves = own.reshape(2, 2, ROWS // 2, columns + LANES)
    own_0 = halves[:, 0].reshape(ROWS, columns + LANES)
    own_1 = halves[:, 1].reshape(ROWS, columns + LANES)
    below_0, above_0 = along_x(own_0, 1), along_x(own_0, -1)
    natural, grouped = (ROWS // 2, ROWS), (2 * ROWS, ROWS // 2)
    codes = [(own, 0), (own, 1), (own_c, 0), (own_c, 1)]
    *sends, kept_0 = product(codes, weight, natural)
    sends, below_0, above_0, own_1 = lax.optimization_barrier((sends, below_0, above_0, own_1))
    below_1, above_1 = along_x(own_1, 1), along_x(own_1, -1)
    got_0 = along_y(sends)
    codes = [above_0, other_core(above_0), below_0, other_core(below_0)]
    *sends, kept_1 = product([(code, 0) for code in codes], weight, grouped)
    sends, below_0, below_1, above_1 = lax.optimization_barrier((sends, below_0, below_1, above_1))
    far_0 = along_x(below_0, 1)
    got_1 = along_y(sends)
    far_1 = along_x(above_1, -1)
    codes = [above_1, other_core(above_1), below_1, other_core(below_1)]
    *sends, kept_2 = product([(code, 0) for code in codes], weight, grouped)
    sends, far_0, far_1 = lax.optimization_barrier((sends, far_0, far_1))
    got_2 = along_y(sends)
    codes = [far_0, other_core(far_0), far_1, other_core(far_1)]
    outs = product([(code, 0) for code in codes], weight, grouped, 2)
    got_a, got_b = along_y(outs[:3]), along_y(outs[4:7])
    *sends, own_a = collect(0, [kept_0, *got_0], [kept_1, *got_1], [outs[3], *got_a])
    end_a = along_z(sends)
    *sends, own_b = collect(1, [kept_0, *got_0], [kept_2, *got_2], [outs[7], *got_b])
    end_b = along_z(sends)
    mixed = finish(w_scale[None, :], [own_a, *end_a, own_b, *end_b])
    return (mixed, act_scale)


def solution(mesh):
    return jax.shard_map(
        step,
        mesh=mesh,
        in_specs=(P("seq", "tensor"), P("tensor", "seq"), P("seq"), P()),
        out_specs=(P("tensor", "seq"), P("seq")),
        check_vma=False,
    )
```
